768 devices in a mesh: dp: 48 (over z_lo, x, core), tensor: 16 (over z_hi, y).
Axes of the slice: x: 4, y: 8, z: 12 (z_hi: 2, z_lo: 6; z = z_hi * 6 + z_lo), core: 2. Of those that a mesh axis runs over, the one named last changes fastest.
Arguments:
- tokens: bfloat16 [24576, 8192], P('dp'), may hold values from -40 to 40
- cotangent: bfloat16 [24576, 2048], P('dp', 'tensor'), may hold values from -260 to 260
- master: float32 [8208, 2048], P('dp', 'tensor'), may hold values from -0.0625 to 0.0625
- first_moment: float32 [8208, 2048], P('dp', 'tensor'), may hold values from -0.0014648438 to 0.0014648438
- second_moment: float32 [8208, 2048], P('dp', 'tensor'), may hold values from 1.7881393e-09 to 1.7881393e-07
- old_rows: int32 [8208], P('dp'), may hold values from 0 to 8207, as said below
Outputs:
- keys_values: bfloat16 [24576, 2048], P('dp', 'tensor')
- update: float32 [8208, 2048], P('dp', 'tensor')
The draws below stay inside these ranges and needn't reach their ends.
Inputs may be any that keep to these rules, and one draw needn't show every extreme that they name: `old_rows`: every row 0 to 8207 is named by exactly one slot. Rows j * 171 to (j + 1) * 171 - 1 belong to new owner j; the slots of one device name at most 8 rows of one owner.
All inputs are finite; a program needn't handle non-finite values.
Results may differ from the reference program's by a relative error of at most 0.0049.
Values may be sent and summed in bfloat16 or wider, within the bound.
No kernel may reach another device: no remote copies, remote signals or barrier semaphores. Data moves between devices by JAX's collectives and lax.ppermute only.
A program may use at most 64 MiB of HBM per device.

```python
import math
import jax
import jax.numpy as jnp

D = 8192
TOK_DEV = 512
KVC = 2048
ROWS_DEV = 171
ROWS = 8208
TOKENS = 24576


def mixed_noise(key, rows, width):
    first, third = jax.random.split(key, 2)
    blocks = rows // TOK_DEV
    noise = jax.random.truncated_normal(first, -6.0, 6.0, (blocks, TOK_DEV, width), jnp.float32)
    local = jax.random.truncated_normal(third, -4.0, 4.0, (blocks, 1, width), jnp.float32)
    mixed = 0.937 * noise + 0.35 * local
    return mixed.reshape(rows, width)


def draw_tokens(key, part):
    base = jax.random.fold_in(key, 101)
    first, second = jax.random.split(base)
    noise = mixed_noise(first, TOKENS, D)
    ramp = jnp.arange(D, dtype=jnp.float32) / (D - 1)
    column = 3.0 ** ramp
    row = 0.35 * 3.0 ** jax.random.uniform(second, (TOKENS, 1), jnp.float32)
    return (noise * column[None, :] * row).astype(jnp.bfloat16)


def draw_cotangent(key, part):
    base = jax.random.fold_in(key, 202)
    first, second = jax.random.split(base)
    noise = mixed_noise(first, TOKENS, KVC)
    column = 3.0 ** (jnp.arange(KVC, dtype=jnp.float32) / (KVC - 1))
    row = 10.0 ** jax.random.uniform(second, (TOKENS, 1), jnp.float32)
    return (noise * column[None, :] * row).astype(jnp.bfloat16)


def draw_old_rows(key, part):
    rows_dev = ROWS_DEV
    peers = ROWS // ROWS_DEV
    base = jax.random.fold_in(key, 303)
    key_split, key_offset, key_order, key_slots = jax.random.split(base, 4)
    whole = rows_dev // peers
    spare = rows_dev % peers
    halves = peers // 2
    pair_ids = jnp.arange(halves, dtype=jnp.int32)
    extra = jnp.clip(spare - 2 * pair_ids, 0, 2)
    pair_total = 2 * whole + extra
    first_size = jax.random.randint(key_split, (halves,), 0, pair_total + 1)
    first_size = jnp.where(pair_ids == 0, pair_total, first_size)
    sizes = jnp.stack([first_size, pair_total - first_size], axis=1).reshape(peers).astype(jnp.int32)
    prefix = (jnp.cumsum(sizes) - sizes).astype(jnp.int32)
    offsets = jax.random.permutation(key_offset, peers).astype(jnp.int32)
    order = jax.random.permutation(key_order, peers).astype(jnp.int32)
    order_back = jnp.argsort(order).astype(jnp.int32)
    class_sorted = jnp.repeat(jnp.arange(peers, dtype=jnp.int32), sizes, total_repeat_length=rows_dev)
    rank_sorted = jnp.arange(rows_dev, dtype=jnp.int32) - prefix[class_sorted]

    def one_device(device):
        shuffle = jax.random.permutation(jax.random.fold_in(key_slots, device), rows_dev)
        classes = class_sorted[shuffle]
        ranks = rank_sorted[shuffle]
        owners = order[(order_back[device] + offsets[classes]) % peers]
        return owners * rows_dev + prefix[classes] + ranks
    table = jax.vmap(one_device)(jnp.arange(peers, dtype=jnp.int32))
    return table.reshape(peers * rows_dev).astype(jnp.int32)


def level_of(key, extent, cuts, low, top_value):
    gain = 1.0
    for position, blocks in cuts:
        steps = jax.random.uniform(jax.random.fold_in(jax.random.fold_in(key, 6), position), (blocks,), jnp.float32, low / len(cuts), top_value / len(cuts))
        gain = gain * jnp.repeat(jnp.exp(steps), extent[position] // blocks).reshape((-1,) + (1,) * (len(extent) - 1 - position))
    return gain


def gaussian(key, dims, deviation, reach, shards=(), kind=jnp.bfloat16):
    array = jax.random.normal(key, dims, jnp.float32) * deviation
    if len(shards) > 0:
        array = level_of(key, dims, shards, -0.22, 0.18) * array
    return jnp.clip(array, min=-reach, max=reach).astype(kind)


def setup_inputs(seed: int = 0) -> dict:
    splits = jax.random.split(jax.random.key(seed), 7)
    return {
        "tokens": draw_tokens(jax.random.fold_in(splits[6], 71), 0),
        "cotangent": draw_cotangent(jax.random.fold_in(splits[6], 71), 0),
        "master": gaussian(splits[2], (ROWS, KVC), D ** -0.5, 0.0625, ((0, 48), (1, 16)), jnp.float32),
        "first_moment": gaussian(splits[3], (ROWS, KVC), (1.0 / (D * KVC) ** 0.5), 0.0014648438, ((0, 48), (1, 16)), jnp.float32),
        "second_moment": jnp.clip(jnp.exp(math.log(1.7881393432617188e-07) - 4.6051702 * jax.random.uniform(splits[4], (ROWS, KVC), jnp.float32) ** level_of(splits[4], (ROWS, KVC), ((0, 48), (1, 16)), -0.2, 0.2)), 1.7881393032936899e-09, 1.7881393432617188e-07),
        "old_rows": draw_old_rows(jax.random.fold_in(splits[6], 71), 0),
    }


beta_one = 0.9
beta_two = 0.95
adam_eps = 1e-08
clip_norm = 1.0

def reference(tokens, cotangent, master, first_moment, second_moment, old_rows):
    new_master = jnp.zeros_like(master).at[old_rows].set(master)
    new_first = jnp.zeros_like(first_moment).at[old_rows].set(first_moment)
    new_second = jnp.zeros_like(second_moment).at[old_rows].set(second_moment)
    weight = new_master[:D].astype(jnp.bfloat16)
    keys_values = jnp.dot(tokens, weight, preferred_element_type=jnp.float32).astype(jnp.bfloat16)
    gradient = jnp.dot(tokens.T, cotangent, preferred_element_type=jnp.float32)
    gradient = jnp.concatenate([gradient, jnp.zeros((ROWS - D, KVC), jnp.float32)], axis=0)
    squares = jnp.sum(gradient * gradient)
    factor = clip_norm / (jnp.sqrt(squares) + 1e-06)
    clipped = gradient * factor
    moment_one = beta_one * new_first + (1.0 - beta_one) * clipped
    moment_two = beta_two * new_second + (1.0 - beta_two) * clipped * clipped
    update = moment_one / (jnp.sqrt(moment_two) + adam_eps)
    return (keys_values, update)
```

```python
import functools

import jax
import jax.numpy as jnp
from jax import lax
from jax.experimental import pallas as pl
from jax.experimental.pallas import tpu as pltpu
from jax.sharding import PartitionSpec as P

beta_one = 0.9
beta_two = 0.95
adam_eps = 1e-08
clip_norm = 1.0

F32, BF16 = jnp.float32, jnp.bfloat16
NZ, NX, NC = 6, 4, 2
DP = NZ * NX * NC
CAP = 8
PAD = 176


SEND_ORDER = (
    [(2, r) for r in (0, 1, 2)]
    + [(1, r) for r in (3, 4, 5)]
    + [(2, r) for r in (3, 4, 5)]
    + [(3, r) for r in (0, 1, 2)]
    + [(1, r) for r in (0, 1, 2)]
    + [(3, r) for r in (3, 4, 5)]
    + [(0, r) for r in range(6)]
)


def shift_pairs(dz, dx, dc):
    pairs = []
    for z in range(NZ):
        for x in range(NX):
            for c in range(NC):
                source = (z * NX + x) * NC + c
                target = (((z + dz) % NZ) * NX + (x + dx) % NX) * NC + (c + dc) % NC
                pairs.append((source, target))
    return pairs


def shift(value, dz=0, dx=0, dc=0):
    return lax.ppermute(value, "dp", shift_pairs(dz, dx, dc))


def iota(shape, axis):
    return lax.broadcasted_iota(jnp.int32, shape, axis).astype(F32)


def route_kernel(rows_ref, master_ref, first_ref, second_ref, out_ref):
    count = rows_ref.shape[1]
    rows_dev = float(count)
    along = rows_ref[...].astype(F32)
    line, column = iota((count, count), 0), iota((count, count), 1)
    down = jnp.sum(jnp.where(line == column, along, 0.0), axis=1, keepdims=True)
    owner_down = jnp.sum(
        jnp.where(down >= rows_dev * (iota((count, 128), 1) + 1.0), 1.0, 0.0), axis=1, keepdims=True
    )
    owner_along = jnp.sum(
        jnp.where(along >= rows_dev * (iota((DP, count), 0) + 1.0), 1.0, 0.0), axis=0, keepdims=True
    )
    before = jnp.where((owner_down == owner_along) & (line < column), 1.0, 0.0)
    within = jnp.sum(before, axis=0, keepdims=True)
    code = owner_along * CAP + within
    pick = jnp.where(code == iota((DP * CAP, count), 0), 1.0, 0.0).astype(BF16)
    label = jnp.broadcast_to(down - rows_dev * owner_down + 1.0, (count, 128))
    data = jnp.concatenate(
        [master_ref[...], first_ref[...], second_ref[...], label], axis=1
    ).astype(BF16)
    sent = jnp.dot(pick, data, preferred_element_type=F32)
    parts = [sent[:, 128 * k : 128 * k + 128].reshape(DP, CAP, 128) for k in range(4)]
    out_ref[...] = jnp.concatenate(parts, axis=1).astype(BF16)


def route(rows, master, first, second):
    return pl.pallas_call(
        route_kernel,
        out_shape=jax.ShapeDtypeStruct((DP, 4 * CAP, 128), BF16),
        name="route",
    )(rows.reshape(1, -1), master, first, second)


def place_kernel(box_ref, weight_ref, first_ref, second_ref):
    box = box_ref[...].astype(F32)
    parts = [box[:, CAP * k : CAP * k + CAP, :].reshape(DP * CAP, 128) for k in range(4)]
    label = parts[3]
    lane = iota((DP * CAP, 128), 1)
    pick = jnp.concatenate(
        [jnp.where(label == lane + 1.0, 1.0, 0.0), jnp.where(label == lane + 129.0, 1.0, 0.0)],
        axis=1,
    ).astype(BF16)
    data = jnp.concatenate(parts[:3], axis=1).astype(BF16)
    placed = lax.dot_general(
        pick, data, (((0,), (0,)), ((), ())), preferred_element_type=F32
    )
    weight_ref[...] = placed[:PAD, :128].astype(BF16)
    first_ref[...] = placed[:PAD, 128:256]
    second_ref[...] = placed[:PAD, 256:384]


def place(box):
    return pl.pallas_call(
        place_kernel,
        out_shape=(
            jax.ShapeDtypeStruct((PAD, 128), BF16),
            jax.ShapeDtypeStruct((PAD, 128), F32),
            jax.ShapeDtypeStruct((PAD, 128), F32),
        ),
        name="place",
    )(box)


def cut_kernel(rows_dev, table_ref, whole_ref, send_ref, keep_ref):
    total = whole_ref.shape[0]
    last = (DP - 1) * rows_dev

    def piece(target, index, start):
        @pl.when(start < last)
        def _():
            target[index] = whole_ref[pl.ds(start, PAD), :].astype(target.dtype)

        @pl.when(start >= last)
        def _():
            tail = jnp.concatenate(
                [whole_ref[last:total, :], jnp.zeros((PAD - (total - last), 128), F32)], axis=0
            )
            target[index] = tail.astype(target.dtype)

    def step(index, carry):
        piece(send_ref, index, table_ref[index])
        piece(keep_ref, index, table_ref[24 + index])
        return carry

    lax.fori_loop(0, 24, step, 0)


def cut(table, whole, rows_dev):
    return pl.pallas_call(
        functools.partial(cut_kernel, rows_dev),
        out_shape=(
            jax.ShapeDtypeStruct((24, PAD, 128), BF16),
            jax.ShapeDtypeStruct((24, PAD, 128), F32),
        ),
        in_specs=[
            pl.BlockSpec(memory_space=pltpu.SMEM),
            pl.BlockSpec(memory_space=pltpu.VMEM),
        ],
        name="cut",
    )(table, whole)


def join_kernel(rows_dev, table_ref, mine_ref, other_ref, out_ref, rows_ref):
    for owner in range(DP):
        index = table_ref[owner]
        place_at = slice(owner * rows_dev, owner * rows_dev + PAD)

        @pl.when(index < 24)
        def _():
            rows_ref[place_at, :] = mine_ref[index].astype(F32)

        @pl.when(index >= 24)
        def _():
            rows_ref[place_at, :] = other_ref[index - 24].astype(F32)

    out_ref[...] = rows_ref[: out_ref.shape[0], :].astype(BF16)


def join(table, mine, other, features, rows_dev):
    return pl.pallas_call(
        functools.partial(join_kernel, rows_dev),
        out_shape=jax.ShapeDtypeStruct((features, 128), BF16),
        in_specs=[
            pl.BlockSpec(memory_space=pltpu.SMEM),
            pl.BlockSpec(memory_space=pltpu.VMEM),
            pl.BlockSpec(memory_space=pltpu.VMEM),
        ],
        scratch_shapes=[pltpu.VMEM((8224, 128), F32)],
        name="join",
    )(table, mine, other)


def per_device(tokens, cotangent, master, first_moment, second_moment, old_rows):
    rows_dev = master.shape[0]
    features = tokens.shape[1]
    me = lax.axis_index("dp")
    my_z, my_x, my_c = me // (NX * NC), (me // NC) % NX, me % NC

    box = route(old_rows, master, first_moment, second_moment)
    arrived = lax.all_to_all(box, "dp", split_axis=0, concat_axis=0, tiled=True)
    weight_own, first, second = place(arrived)

    whole = lax.dot_general(
        tokens, cotangent, (((0,), (0,)), ((), ())), preferred_element_type=F32
    )
    step_x = jnp.array([k for k, r in SEND_ORDER], jnp.int32)
    step_z = jnp.array([r for k, r in SEND_ORDER], jnp.int32)
    chip = ((my_z + step_z) % NZ) * NX + (my_x + step_x) % NX
    starts = jnp.concatenate([chip * NC + (1 - my_c), chip * NC + my_c]) * rows_dev
    send, keep = cut(starts, whole, rows_dev)
    got = shift(send, dc=1)
    right = (keep[0:6] + got[0:6].astype(F32)).astype(BF16)
    left = (keep[6:12] + got[6:12].astype(F32)).astype(BF16)
    from_left, from_right = shift(right, dx=1), shift(left, dx=-1)
    right_two = keep[12:15] + got[12:15].astype(F32) + from_left[0:3].astype(F32)
    left_two = keep[15:18] + got[15:18].astype(F32) + from_right[0:3].astype(F32)
    from_left_two = shift(right_two.astype(BF16), dx=1)
    from_right_two = shift(left_two.astype(BF16), dx=-1)
    near = (
        keep[18:21]
        + got[18:21].astype(F32)
        + from_right[3:6].astype(F32)
        + from_left_two.astype(F32)
    )
    far = (
        keep[21:24]
        + got[21:24].astype(F32)
        + from_left[3:6].astype(F32)
        + from_right_two.astype(F32)
    )
    pieces = [near[0], near[1], near[2], far[0], far[1], far[2]]
    gradient = pieces[0]
    for r in range(1, NZ):
        gradient = gradient + shift(pieces[r].astype(BF16), dz=r).astype(F32)
    gradient = gradient[:rows_dev]

    squares = jnp.sum(gradient * gradient)
    parts = lax.all_to_all(
        jnp.broadcast_to(squares, (DP, 1, 128)), "dp", split_axis=0, concat_axis=0, tiled=True
    )
    squares = jnp.sum(parts[:, 0, 0])
    tensor = lax.axis_size("tensor")
    parts = lax.all_to_all(
        jnp.broadcast_to(squares, (tensor, 1, 128)), "tensor", split_axis=0, concat_axis=0, tiled=True
    )
    squares = jnp.sum(parts[:, 0, 0])

    run = jnp.stack([weight_own] + [shift(weight_own, dz=r) for r in range(1, NZ)])
    west, east = shift(run, dx=1), shift(run, dx=-1)
    across_a, across_b = shift(west[0:3], dx=1), shift(east[3:6], dx=-1)
    mine = jnp.concatenate([run, west, east, across_a, across_b], axis=0)
    other = shift(mine, dc=1)
    owner = jnp.arange(DP, dtype=jnp.int32)
    back_z = (my_z - owner // (NX * NC)) % NZ
    back_x = (my_x - (owner // NC) % NX) % NX
    group = jnp.where(back_x == 0, 0, jnp.where(back_x == 1, 6, jnp.where(back_x == 3, 12, 18)))
    where = group + back_z + jnp.where(owner % NC == my_c, 0, 24)
    weight = join(where, mine, other, features, rows_dev)
    keys_values = jnp.dot(tokens, weight, preferred_element_type=F32).astype(BF16)

    factor = clip_norm / (jnp.sqrt(squares) + 1e-06)
    clipped = gradient * factor
    moment_one = beta_one * first[:rows_dev] + (1.0 - beta_one) * clipped
    moment_two = beta_two * second[:rows_dev] + (1.0 - beta_two) * clipped * clipped
    update = moment_one / (jnp.sqrt(moment_two) + adam_eps)
    return (keys_values, update)


def solution(mesh):
    in_specs = (
        P("dp", None),
        P("dp", "tensor"),
        P("dp", "tensor"),
        P("dp", "tensor"),
        P("dp", "tensor"),
        P("dp"),
    )
    out_specs = (P("dp", "tensor"), P("dp", "tensor"))
    return jax.shard_map(
        per_device, mesh=mesh, in_specs=in_specs, out_specs=out_specs, check_vma=False
    )
```

```python
import functools

import jax
import jax.numpy as jnp
from jax import lax
from jax.experimental import pallas as pl
from jax.experimental.pallas import tpu as pltpu
from jax.sharding import PartitionSpec as P

beta_one = 0.9
beta_two = 0.95
adam_eps = 1e-08
clip_norm = 1.0

F32, BF16 = jnp.float32, jnp.bfloat16
NZ, NX, NC = 6, 4, 2
DP = NZ * NX * NC
CAP = 8
PAD = 176


SEND_ORDER = (
    [(2, r) for r in (0, 1, 2)]
    + [(1, r) for r in (3, 4, 5)]
    + [(2, r) for r in (3, 4, 5)]
    + [(3, r) for r in (0, 1, 2)]
    + [(1, r) for r in (0, 1, 2)]
    + [(3, r) for r in (3, 4, 5)]
    + [(0, r) for r in range(6)]
)


def shift_pairs(da, db, dx, dc):
    pairs = []
    for z in range(NZ):
        for x in range(NX):
            for c in range(NC):
                source = (z * NX + x) * NC + c
                to_z = (z + 2 * da) % NZ ^ db
                target = (to_z * NX + (x + dx) % NX) * NC + (c + dc) % NC
                pairs.append((source, target))
    return pairs


def shift(value, da=0, db=0, dx=0, dc=0):
    return lax.ppermute(value, "dp", shift_pairs(da, db, dx, dc))


def swap(value, bit):
    size = lax.axis_size("tensor")
    return lax.ppermute(value, "tensor", [(i, i ^ bit) for i in range(size)])


def iota(shape, axis):
    return lax.broadcasted_iota(jnp.int32, shape, axis).astype(F32)


def route_kernel(rows_ref, master_ref, first_ref, second_ref, out_ref):
    count = rows_ref.shape[1]
    rows_dev = float(count)
    along = rows_ref[...].astype(F32)
    line, column = iota((count, count), 0), iota((count, count), 1)
    down = jnp.sum(jnp.where(line == column, along, 0.0), axis=1, keepdims=True)
    owner_down = jnp.sum(
        jnp.where(down >= rows_dev * (iota((count, 128), 1) + 1.0), 1.0, 0.0), axis=1, keepdims=True
    )
    owner_along = jnp.sum(
        jnp.where(along >= rows_dev * (iota((DP, count), 0) + 1.0), 1.0, 0.0), axis=0, keepdims=True
    )
    before = jnp.where((owner_down == owner_along) & (line < column), 1.0, 0.0)
    within = jnp.sum(before, axis=0, keepdims=True)
    code = owner_along * CAP + within
    pick = jnp.where(code == iota((DP * CAP, count), 0), 1.0, 0.0).astype(BF16)
    label = jnp.broadcast_to(down - rows_dev * owner_down + 1.0, (count, 128))
    data = jnp.concatenate(
        [master_ref[...], first_ref[...], second_ref[...], label], axis=1
    ).astype(BF16)
    sent = jnp.dot(pick, data, preferred_element_type=F32)
    parts = [sent[:, 128 * k : 128 * k + 128].reshape(DP, CAP, 128) for k in range(4)]
    out_ref[...] = jnp.concatenate(parts, axis=1).astype(BF16)


def route(rows, master, first, second):
    return pl.pallas_call(
        route_kernel,
        out_shape=jax.ShapeDtypeStruct((DP, 4 * CAP, 128), BF16),
        name="route",
    )(rows.reshape(1, -1), master, first, second)


def place_kernel(box_ref, weight_ref, first_ref, second_ref):
    box = box_ref[...].astype(F32)
    parts = [box[:, CAP * k : CAP * k + CAP, :].reshape(DP * CAP, 128) for k in range(4)]
    label = parts[3]
    lane = iota((DP * CAP, 128), 1)
    pick = jnp.concatenate(
        [jnp.where(label == lane + 1.0, 1.0, 0.0), jnp.where(label == lane + 129.0, 1.0, 0.0)],
        axis=1,
    ).astype(BF16)
    data = jnp.concatenate(parts[:3], axis=1).astype(BF16)
    placed = lax.dot_general(
        pick, data, (((0,), (0,)), ((), ())), preferred_element_type=F32
    )
    weight_ref[...] = placed[:PAD, :128].astype(BF16)
    first_ref[...] = placed[:PAD, 128:256]
    second_ref[...] = placed[:PAD, 256:384]


def place(box):
    return pl.pallas_call(
        place_kernel,
        out_shape=(
            jax.ShapeDtypeStruct((PAD, 128), BF16),
            jax.ShapeDtypeStruct((PAD, 128), F32),
            jax.ShapeDtypeStruct((PAD, 128), F32),
        ),
        name="place",
    )(box)


def cut_kernel(rows_dev, table_ref, whole_ref, send_ref, keep_ref):
    total = whole_ref.shape[0]
    last = (DP - 1) * rows_dev

    def piece(target, index, start):
        @pl.when(start < last)
        def _():
            target[index] = whole_ref[pl.ds(start, PAD), :].astype(target.dtype)

        @pl.when(start >= last)
        def _():
            tail = jnp.concatenate(
                [whole_ref[last:total, :], jnp.zeros((PAD - (total - last), 128), F32)], axis=0
            )
            target[index] = tail.astype(target.dtype)

    def step(index, carry):
        piece(send_ref, index, table_ref[index])
        piece(keep_ref, index, table_ref[24 + index])
        return carry

    lax.fori_loop(0, 24, step, 0)


def cut(table, whole, rows_dev):
    return pl.pallas_call(
        functools.partial(cut_kernel, rows_dev),
        out_shape=(
            jax.ShapeDtypeStruct((24, PAD, 128), BF16),
            jax.ShapeDtypeStruct((24, PAD, 128), F32),
        ),
        in_specs=[
            pl.BlockSpec(memory_space=pltpu.SMEM),
            pl.BlockSpec(memory_space=pltpu.VMEM),
        ],
        name="cut",
    )(table, whole)


def join_kernel(rows_dev, table_ref, mine_ref, other_ref, out_ref, rows_ref):
    for owner in range(DP):
        index = table_ref[owner]
        place_at = slice(owner * rows_dev, owner * rows_dev + PAD)

        @pl.when(index < 24)
        def _():
            rows_ref[place_at, :] = mine_ref[index].astype(F32)

        @pl.when(index >= 24)
        def _():
            rows_ref[place_at, :] = other_ref[index - 24].astype(F32)

    out_ref[...] = rows_ref[: out_ref.shape[0], :].astype(BF16)


def join(table, mine, other, features, rows_dev):
    return pl.pallas_call(
        functools.partial(join_kernel, rows_dev),
        out_shape=jax.ShapeDtypeStruct((features, 128), BF16),
        in_specs=[
            pl.BlockSpec(memory_space=pltpu.SMEM),
            pl.BlockSpec(memory_space=pltpu.VMEM),
            pl.BlockSpec(memory_space=pltpu.VMEM),
        ],
        scratch_shapes=[pltpu.VMEM((8224, 128), F32)],
        name="join",
    )(table, mine, other)


def per_device(tokens, cotangent, master, first_moment, second_moment, old_rows):
    rows_dev = master.shape[0]
    features = tokens.shape[1]
    me = lax.axis_index("dp")
    my_z, my_x, my_c = me // (NX * NC), (me // NC) % NX, me % NC

    box = route(old_rows, master, first_moment, second_moment)
    arrived = lax.all_to_all(box, "dp", split_axis=0, concat_axis=0, tiled=True)
    weight_own, first, second = place(arrived)

    whole = lax.dot_general(
        tokens, cotangent, (((0,), (0,)), ((), ())), preferred_element_type=F32
    )
    step_x = jnp.array([k for k, r in SEND_ORDER], jnp.int32)
    step_z = jnp.array([r for k, r in SEND_ORDER], jnp.int32)
    to_z = (my_z // 2 + step_z % 3) % 3 * 2 + jnp.where(step_z < 3, my_z % 2, 1 - my_z % 2)
    chip = to_z * NX + (my_x + step_x) % NX
    starts = jnp.concatenate([chip * NC + (1 - my_c), chip * NC + my_c]) * rows_dev
    send, keep = cut(starts, whole, rows_dev)
    got = shift(send, dc=1)
    right = (keep[0:6] + got[0:6].astype(F32)).astype(BF16)
    left = (keep[6:12] + got[6:12].astype(F32)).astype(BF16)
    from_left, from_right = shift(right, dx=1), shift(left, dx=-1)
    right_two = keep[12:15] + got[12:15].astype(F32) + from_left[0:3].astype(F32)
    left_two = keep[15:18] + got[15:18].astype(F32) + from_right[0:3].astype(F32)
    right_two, left_two, from_left, from_right = lax.optimization_barrier(
        (right_two.astype(BF16), left_two.astype(BF16), from_left, from_right)
    )
    from_left_two = shift(right_two, dx=1)
    from_right_two = shift(left_two, dx=-1)
    near = (
        keep[18:21]
        + got[18:21].astype(F32)
        + from_right[3:6].astype(F32)
        + from_left_two.astype(F32)
    )
    far = (
        keep[21:24]
        + got[21:24].astype(F32)
        + from_left[3:6].astype(F32)
        + from_right_two.astype(F32)
    )
    near = near + shift(far.astype(BF16), db=1).astype(F32)
    gradient = (
        near[0]
        + shift(near[1].astype(BF16), da=1).astype(F32)
        + shift(near[2].astype(BF16), da=2).astype(F32)
    )[:rows_dev]

    squares = jnp.sum(gradient * gradient)
    high = squares.astype(BF16)
    middle = (squares - high.astype(F32)).astype(BF16)
    low = (squares - high.astype(F32) - middle.astype(F32)).astype(BF16)
    row = lax.broadcasted_iota(jnp.int32, (PAD, 128), 0)
    own = jnp.where(
        row < rows_dev,
        weight_own,
        jnp.where(row == rows_dev, high, jnp.where(row == rows_dev + 1, middle, low)),
    )

    three = jnp.stack([own, shift(own, da=1), shift(own, da=2)])
    run = jnp.concatenate([three, shift(three, db=1)], axis=0)
    west, east = shift(run, dx=1), shift(run, dx=-1)
    across_a, across_b = shift(west[0:3], dx=1), shift(east[3:6], dx=-1)
    mine = jnp.concatenate([run, west, east, across_a, across_b], axis=0)
    other = shift(mine, dc=1)

    ends = slice(rows_dev, rows_dev + 3)
    squares = jnp.sum(mine[:, ends, :].astype(F32) + other[:, ends, :].astype(F32), axis=(0, 1))
    squares = squares.reshape(1, 128)
    for bit in (8, 4, 2, 1):
        squares = squares + swap(squares, bit)
    squares = squares[0, 0]

    owner = jnp.arange(DP, dtype=jnp.int32)
    owner_z = owner // (NX * NC)
    back_z = (my_z // 2 - owner_z // 2) % 3 + jnp.where(owner_z % 2 == my_z % 2, 0, 3)
    back_x = (my_x - (owner // NC) % NX) % NX
    group = jnp.where(back_x == 0, 0, jnp.where(back_x == 1, 6, jnp.where(back_x == 3, 12, 18)))
    where = group + back_z + jnp.where(owner % NC == my_c, 0, 24)
    weight = join(where, mine, other, features, rows_dev)
    keys_values = jnp.dot(tokens, weight, preferred_element_type=F32).astype(BF16)

    factor = clip_norm / (jnp.sqrt(squares) + 1e-06)
    clipped = gradient * factor
    moment_one = beta_one * first[:rows_dev] + (1.0 - beta_one) * clipped
    moment_two = beta_two * second[:rows_dev] + (1.0 - beta_two) * clipped * clipped
    update = moment_one / (jnp.sqrt(moment_two) + adam_eps)
    return (keys_values, update)


def solution(mesh):
    in_specs = (
        P("dp", None),
        P("dp", "tensor"),
        P("dp", "tensor"),
        P("dp", "tensor"),
        P("dp", "tensor"),
        P("dp"),
    )
    out_specs = (P("dp", "tensor"), P("dp", "tensor"))
    return jax.shard_map(
        per_device, mesh=mesh, in_specs=in_specs, out_specs=out_specs, check_vma=False
    )
```

```python
import functools

import jax
import jax.numpy as jnp
from jax import lax
from jax.experimental import pallas as pl
from jax.experimental.pallas import tpu as pltpu
from jax.sharding import PartitionSpec as P

beta_one = 0.9
beta_two = 0.95
adam_eps = 1e-08
clip_norm = 1.0

F32, BF16 = jnp.float32, jnp.bfloat16
NZ, NX, NC = 6, 4, 2
DP = NZ * NX * NC
CAP = 8
PAD = 176
BLOCKS = 8


FIRST, SECOND = (1, 3), (3, 1)


def shift(value, da=0, db=0, dx=(0, 0), dc=0):
    pairs = []
    for z in range(NZ):
        for x in range(NX):
            for c in range(NC):
                source = (z * NX + x) * NC + c
                to_z = (z + 2 * da) % NZ ^ db
                pairs.append((source, (to_z * NX + (x ^ dx[c])) * NC + (c ^ dc)))
    return lax.ppermute(value, "dp", pairs)


def swap(value, bit):
    size = lax.axis_size("tensor")
    return lax.ppermute(value, "tensor", [(i, i ^ bit) for i in range(size)])


def iota(shape, axis):
    return lax.broadcasted_iota(jnp.int32, shape, axis).astype(F32)


def route_kernel(rows_ref, master_ref, first_ref, second_ref, out_ref):
    count = rows_ref.shape[1]
    rows_dev = float(count)
    along = rows_ref[...].astype(F32)
    line, column = iota((count, count), 0), iota((count, count), 1)
    down = jnp.sum(jnp.where(line == column, along, 0.0), axis=1, keepdims=True)
    owner_down = jnp.sum(
        jnp.where(down >= rows_dev * (iota((count, 128), 1) + 1.0), 1.0, 0.0), axis=1, keepdims=True
    )
    owner_along = jnp.sum(
        jnp.where(along >= rows_dev * (iota((DP, count), 0) + 1.0), 1.0, 0.0), axis=0, keepdims=True
    )
    before = jnp.where((owner_down == owner_along) & (line < column), 1.0, 0.0)
    within = jnp.sum(before, axis=0, keepdims=True)
    code = owner_along * CAP + within
    pick = jnp.where(code == iota((DP * CAP, count), 0), 1.0, 0.0).astype(BF16)
    label = jnp.broadcast_to(down - rows_dev * owner_down + 1.0, (count, 128))
    data = jnp.concatenate(
        [master_ref[...], first_ref[...], second_ref[...], label], axis=1
    ).astype(BF16)
    sent = jnp.dot(pick, data, preferred_element_type=F32)
    parts = [sent[:, 128 * k : 128 * k + 128].reshape(DP, CAP, 128) for k in range(4)]
    out_ref[...] = jnp.concatenate(parts, axis=1).astype(BF16)


def route(rows, master, first, second):
    return pl.pallas_call(
        route_kernel,
        out_shape=jax.ShapeDtypeStruct((DP, 4 * CAP, 128), BF16),
        name="route",
    )(rows.reshape(1, -1), master, first, second)


def place_kernel(box_ref, weight_ref, first_ref, second_ref):
    box = box_ref[...].astype(F32)
    parts = [box[:, CAP * k : CAP * k + CAP, :].reshape(DP * CAP, 128) for k in range(4)]
    label = parts[3]
    lane = iota((DP * CAP, 128), 1)
    pick = jnp.concatenate(
        [jnp.where(label == lane + 1.0, 1.0, 0.0), jnp.where(label == lane + 129.0, 1.0, 0.0)],
        axis=1,
    ).astype(BF16)
    data = jnp.concatenate(parts[:3], axis=1).astype(BF16)
    placed = lax.dot_general(
        pick, data, (((0,), (0,)), ((), ())), preferred_element_type=F32
    )
    weight_ref[...] = placed[:PAD, :128].astype(BF16)
    first_ref[...] = placed[:PAD, 128:256]
    second_ref[...] = placed[:PAD, 256:384]


def place(box):
    return pl.pallas_call(
        place_kernel,
        out_shape=(
            jax.ShapeDtypeStruct((PAD, 128), BF16),
            jax.ShapeDtypeStruct((PAD, 128), F32),
            jax.ShapeDtypeStruct((PAD, 128), F32),
        ),
        name="place",
    )(box)


def slot_bits(me_ref):
    me = me_ref[0]
    z = lax.div(me, NX * NC)
    x = lax.rem(lax.div(me, NC), NX)
    return lax.div(z, 2), lax.rem(z, 2), x, lax.rem(me, NC)


def pick_of(key, values):
    chosen = jnp.int32(values[-1])
    for index, value in enumerate(values[:-1]):
        chosen = jnp.where(key == index, jnp.int32(value), chosen)
    return chosen


def fetch(tokens_hbm, tokens_ref, sems):
    width = tokens_ref.shape[1] // BLOCKS
    copies = [
        pltpu.make_async_copy(
            tokens_hbm.at[:, pl.ds(i * width, width)],
            tokens_ref.at[:, pl.ds(i * width, width)],
            sems.at[i],
        )
        for i in range(BLOCKS)
    ]
    for copy in copies:
        copy.start()
    return copies


def grad_kernel(
    rows_dev, me_ref, cot_ref, tokens_hbm, send_ref, keep_ref, tokens_ref, whole_ref, sems
):
    features = tokens_ref.shape[1]
    width = features // BLOCKS
    copies = fetch(tokens_hbm, tokens_ref, sems)
    my_a, my_b, my_x, my_c = slot_bits(me_ref)
    even = my_c == 0
    whole_ref[features:, :] = jnp.zeros((whole_ref.shape[0] - features, 128), F32)
    turned = cot_ref[...].T
    chip = 0
    for i in range(BLOCKS):
        copies[i].wait()
        across = jnp.dot(
            turned, tokens_ref[:, i * width : i * width + width], preferred_element_type=F32
        )
        whole_ref[i * width : i * width + width, :] = across.T
        ready = (i + 1) * width if i < BLOCKS - 1 else whole_ref.shape[0]
        while chip < DP // NC and (2 * chip + 1) * rows_dev + PAD <= ready:
            z, x = chip // NX, chip % NX
            steps_a = lax.rem(z // 2 + 3 - my_a, 3) + jnp.where(my_b == z % 2, 0, 3)
            apart = jnp.bitwise_xor(my_x, x)
            zero, one = pick_of(apart, (18, 6, 0, 12)), pick_of(apart, (18, 12, 0, 6))
            kept = steps_a + jnp.where(even, zero, one)
            sent = steps_a + jnp.where(even, one, zero)
            first = whole_ref[2 * chip * rows_dev : 2 * chip * rows_dev + PAD, :]
            second = whole_ref[(2 * chip + 1) * rows_dev : (2 * chip + 1) * rows_dev + PAD, :]
            keep_ref[kept] = jnp.where(even, first, second)
            send_ref[sent] = jnp.where(even, second, first).astype(BF16)
            chip += 1


def grad(me, cotangent, tokens, rows_dev):
    tall, features = tokens.shape
    return pl.pallas_call(
        functools.partial(grad_kernel, rows_dev),
        out_shape=(
            jax.ShapeDtypeStruct((24, PAD, 128), BF16),
            jax.ShapeDtypeStruct((24, PAD, 128), F32),
        ),
        in_specs=[
            pl.BlockSpec(memory_space=pltpu.SMEM),
            pl.BlockSpec(memory_space=pltpu.VMEM),
            pl.BlockSpec(memory_space=pltpu.HBM),
        ],
        out_specs=[pl.BlockSpec(memory_space=pltpu.VMEM)] * 2,
        scratch_shapes=[
            pltpu.VMEM(tokens.shape, BF16),
            pltpu.VMEM((features + 32, 128), F32),
            pltpu.SemaphoreType.DMA((BLOCKS,)),
        ],
        compiler_params=pltpu.CompilerParams(vmem_limit_bytes=60_000_000),
        name="grad",
    )(me.reshape(1), cotangent, tokens)


def apply_kernel(
    rows_dev, me_ref, mine_ref, other_ref, tokens_hbm, out_ref, tokens_ref, rows_ref, sems
):
    features = tokens_ref.shape[1]
    width = features // BLOCKS
    copies = fetch(tokens_hbm, tokens_ref, sems)
    my_a, my_b, my_x, my_c = slot_bits(me_ref)
    even = my_c == 0
    total = jnp.zeros(out_ref.shape, F32)
    chip = 0
    for i in range(BLOCKS):
        while chip < DP // NC and 2 * chip * rows_dev < (i + 1) * width:
            z, x = chip // NX, chip % NX
            steps_a = lax.rem(my_a + 3 - z // 2, 3) + jnp.where(my_b == z % 2, 0, 3)
            apart = jnp.bitwise_xor(my_x, x)
            zero, one = pick_of(apart, (0, 6, 18, 12)), pick_of(apart, (0, 12, 18, 6))
            mine = mine_ref[steps_a + jnp.where(even, zero, one)].astype(F32)
            other = other_ref[steps_a + jnp.where(even, one, zero)].astype(F32)
            start = 2 * chip * rows_dev
            rows_ref[start : start + PAD, :] = jnp.where(even, mine, other)
            start += rows_dev
            rows_ref[start : start + PAD, :] = jnp.where(even, other, mine)
            chip += 1
        block = slice(i * width, i * width + width)
        copies[i].wait()
        total += jnp.dot(
            tokens_ref[:, block], rows_ref[block, :].astype(BF16), preferred_element_type=F32
        )
    out_ref[...] = total.astype(BF16)


def apply(me, mine, other, tokens, rows_dev):
    tall, features = tokens.shape
    return pl.pallas_call(
        functools.partial(apply_kernel, rows_dev),
        out_shape=jax.ShapeDtypeStruct((tall, 128), BF16),
        in_specs=[pl.BlockSpec(memory_space=pltpu.SMEM)]
        + [pl.BlockSpec(memory_space=pltpu.VMEM)] * 2
        + [pl.BlockSpec(memory_space=pltpu.HBM)],
        scratch_shapes=[
            pltpu.VMEM(tokens.shape, BF16),
            pltpu.VMEM((features + 32, 128), F32),
            pltpu.SemaphoreType.DMA((BLOCKS,)),
        ],
        compiler_params=pltpu.CompilerParams(vmem_limit_bytes=60_000_000),
        name="apply",
    )(me.reshape(1), mine, other, tokens)


def per_device(tokens, cotangent, master, first_moment, second_moment, old_rows):
    rows_dev = master.shape[0]
    me = lax.axis_index("dp")

    box = route(old_rows, master, first_moment, second_moment)
    arrived = lax.all_to_all(box, "dp", split_axis=0, concat_axis=0, tiled=True)
    weight_own, first, second = place(arrived)

    send, keep = grad(me, cotangent, tokens, rows_dev)
    got = shift(send, dc=1)
    got_x = shift((keep[:12] + got[:12].astype(F32)).astype(BF16), dx=FIRST)
    next_x = keep[12:18] + got[12:18].astype(F32) + got_x[:6].astype(F32)
    next_x, got_x = lax.optimization_barrier((next_x.astype(BF16), got_x))
    last_x = shift(next_x, dx=SECOND)
    sums = (
        keep[18:] + got[18:].astype(F32) + got_x[6:].astype(F32) + last_x.astype(F32)
    )
    near, far = sums[:3], sums[3:]
    near = near + shift(far.astype(BF16), db=1).astype(F32)
    gradient = (
        near[0]
        + shift(near[1].astype(BF16), da=1).astype(F32)
        + shift(near[2].astype(BF16), da=2).astype(F32)
    )[:rows_dev]

    squares = jnp.sum(gradient * gradient)
    high = squares.astype(BF16)
    middle = (squares - high.astype(F32)).astype(BF16)
    low = (squares - high.astype(F32) - middle.astype(F32)).astype(BF16)
    row = lax.broadcasted_iota(jnp.int32, (PAD, 128), 0)
    own = jnp.where(
        row < rows_dev,
        weight_own,
        jnp.where(row == rows_dev, high, jnp.where(row == rows_dev + 1, middle, low)),
    )

    three = jnp.stack([own, shift(own, da=1), shift(own, da=2)])
    run = jnp.concatenate([three, shift(three, db=1)], axis=0)
    pair = jnp.concatenate([run, shift(run, dx=FIRST)], axis=0)
    mine = jnp.concatenate([pair, shift(pair, dx=SECOND)], axis=0)
    other = shift(mine, dc=1)

    ends = slice(rows_dev, rows_dev + 3)
    squares = jnp.sum(mine[:, ends, :].astype(F32) + other[:, ends, :].astype(F32), axis=(0, 1))
    squares = squares.reshape(1, 128)
    squares = squares + swap(squares, 8)
    half = lax.axis_size("tensor") // 2
    groups = [list(range(half)), list(range(half, 2 * half))]
    squares = lax.psum(squares, "tensor", axis_index_groups=groups)[0, 0]

    keys_values = apply(me, mine, other, tokens, rows_dev)

    factor = clip_norm / (jnp.sqrt(squares) + 1e-06)
    clipped = gradient * factor
    moment_one = beta_one * first[:rows_dev] + (1.0 - beta_one) * clipped
    moment_two = beta_two * second[:rows_dev] + (1.0 - beta_two) * clipped * clipped
    update = moment_one / (jnp.sqrt(moment_two) + adam_eps)
    return (keys_values, update)


def solution(mesh):
    in_specs = (
        P("dp", None),
        P("dp", "tensor"),
        P("dp", "tensor"),
        P("dp", "tensor"),
        P("dp", "tensor"),
        P("dp"),
    )
    out_specs = (P("dp", "tensor"), P("dp", "tensor"))
    return jax.shard_map(
        per_device, mesh=mesh, in_specs=in_specs, out_specs=out_specs, check_vma=False
    )
```

```python
import functools

import jax
import jax.numpy as jnp
from jax import lax
from jax.experimental import pallas as pl
from jax.experimental.pallas import tpu as pltpu
from jax.sharding import PartitionSpec as P

beta_one = 0.9
beta_two = 0.95
adam_eps = 1e-08
clip_norm = 1.0

F32, BF16 = jnp.float32, jnp.bfloat16
NZ, NX, NC = 6, 4, 2
DP = NZ * NX * NC
CAP = 8
PAD = 176
BLOCKS = 8


FIRST, SECOND = (1, 3), (3, 1)


def shift(value, da=0, db=0, dx=(0, 0), dc=0):
    pairs = []
    for z in range(NZ):
        for x in range(NX):
            for c in range(NC):
                source = (z * NX + x) * NC + c
                to_z = (z + 2 * da) % NZ ^ db
                pairs.append((source, (to_z * NX + (x ^ dx[c])) * NC + (c ^ dc)))
    return lax.ppermute(value, "dp", pairs)


def swap(value, bit):
    size = lax.axis_size("tensor")
    return lax.ppermute(value, "tensor", [(i, i ^ bit) for i in range(size)])


def iota(shape, axis):
    return lax.broadcasted_iota(jnp.int32, shape, axis).astype(F32)


def route_kernel(rows_ref, master_ref, first_ref, second_ref, out_ref):
    count = rows_ref.shape[1]
    rows_dev = float(count)
    along = rows_ref[...].astype(F32)
    line, column = iota((count, count), 0), iota((count, count), 1)
    down = jnp.sum(jnp.where(line == column, along, 0.0), axis=1, keepdims=True)
    owner_down = jnp.sum(
        jnp.where(down >= rows_dev * (iota((count, 128), 1) + 1.0), 1.0, 0.0), axis=1, keepdims=True
    )
    owner_along = jnp.sum(
        jnp.where(along >= rows_dev * (iota((DP, count), 0) + 1.0), 1.0, 0.0), axis=0, keepdims=True
    )
    before = jnp.where((owner_down == owner_along) & (line < column), 1.0, 0.0)
    within = jnp.sum(before, axis=0, keepdims=True)
    code = owner_along * CAP + within
    pick = jnp.where(code == iota((DP * CAP, count), 0), 1.0, 0.0).astype(BF16)
    label = jnp.broadcast_to(down - rows_dev * owner_down + 1.0, (count, 128))
    data = jnp.concatenate(
        [master_ref[...], first_ref[...], second_ref[...], label], axis=1
    ).astype(BF16)
    sent = jnp.dot(pick, data, preferred_element_type=F32)
    parts = [sent[:, 128 * k : 128 * k + 128].reshape(DP, CAP, 128) for k in range(4)]
    out_ref[...] = jnp.concatenate(parts, axis=1).astype(BF16)


def route(rows, master, first, second):
    return pl.pallas_call(
        route_kernel,
        out_shape=jax.ShapeDtypeStruct((DP, 4 * CAP, 128), BF16),
        name="route",
    )(rows.reshape(1, -1), master, first, second)


def place_kernel(box_ref, weight_ref, first_ref, second_ref):
    box = box_ref[...].astype(F32)
    parts = [box[:, CAP * k : CAP * k + CAP, :].reshape(DP * CAP, 128) for k in range(4)]
    label = parts[3]
    lane = iota((DP * CAP, 128), 1)
    pick = jnp.concatenate(
        [jnp.where(label == lane + 1.0, 1.0, 0.0), jnp.where(label == lane + 129.0, 1.0, 0.0)],
        axis=1,
    ).astype(BF16)
    data = jnp.concatenate(parts[:3], axis=1).astype(BF16)
    placed = lax.dot_general(
        pick, data, (((0,), (0,)), ((), ())), preferred_element_type=F32
    )
    weight_ref[...] = placed[:PAD, :128].astype(BF16)
    first_ref[...] = placed[:PAD, 128:256]
    second_ref[...] = placed[:PAD, 256:384]


def place(box):
    return pl.pallas_call(
        place_kernel,
        out_shape=(
            jax.ShapeDtypeStruct((PAD, 128), BF16),
            jax.ShapeDtypeStruct((PAD, 128), F32),
            jax.ShapeDtypeStruct((PAD, 128), F32),
        ),
        name="place",
    )(box)


def slot_bits(me_ref):
    me = me_ref[0]
    z = lax.div(me, NX * NC)
    x = lax.rem(lax.div(me, NC), NX)
    return lax.div(z, 2), lax.rem(z, 2), x, lax.rem(me, NC)


def pick_of(key, values):
    chosen = jnp.int32(values[-1])
    for index, value in enumerate(values[:-1]):
        chosen = jnp.where(key == index, jnp.int32(value), chosen)
    return chosen


def fetch(tokens_hbm, tokens_ref, sems):
    width = tokens_ref.shape[1] // BLOCKS
    copies = [
        pltpu.make_async_copy(
            tokens_hbm.at[:, pl.ds(i * width, width)],
            tokens_ref.at[:, pl.ds(i * width, width)],
            sems.at[i],
        )
        for i in range(BLOCKS)
    ]
    for copy in copies:
        copy.start()
    return copies


def grad_kernel(
    rows_dev, me_ref, cot_ref, tokens_hbm, send_ref, keep_ref, tokens_ref, whole_ref, sems
):
    features = tokens_ref.shape[1]
    width = features // BLOCKS
    copies = fetch(tokens_hbm, tokens_ref, sems)
    my_a, my_b, my_x, my_c = slot_bits(me_ref)
    even = my_c == 0
    whole_ref[features:, :] = jnp.zeros((whole_ref.shape[0] - features, 128), F32)
    turned = cot_ref[...].T
    chip = 0
    for i in range(BLOCKS):
        copies[i].wait()
        across = jnp.dot(
            turned, tokens_ref[:, i * width : i * width + width], preferred_element_type=F32
        )
        whole_ref[i * width : i * width + width, :] = across.T
        ready = (i + 1) * width if i < BLOCKS - 1 else whole_ref.shape[0]
        while chip < DP // NC and (2 * chip + 1) * rows_dev + PAD <= ready:
            z, x = chip // NX, chip % NX
            steps_a = lax.rem(z // 2 + 3 - my_a, 3) + jnp.where(my_b == z % 2, 0, 3)
            apart = jnp.bitwise_xor(my_x, x)
            zero, one = pick_of(apart, (18, 6, 0, 12)), pick_of(apart, (18, 12, 0, 6))
            kept = steps_a + jnp.where(even, zero, one)
            sent = steps_a + jnp.where(even, one, zero)
            first = whole_ref[2 * chip * rows_dev : 2 * chip * rows_dev + PAD, :]
            second = whole_ref[(2 * chip + 1) * rows_dev : (2 * chip + 1) * rows_dev + PAD, :]
            keep_ref[kept] = jnp.where(even, first, second)
            send_ref[sent] = jnp.where(even, second, first).astype(BF16)
            chip += 1


def grad(me, cotangent, tokens, rows_dev):
    _, features = tokens.shape
    return pl.pallas_call(
        functools.partial(grad_kernel, rows_dev),
        out_shape=(
            jax.ShapeDtypeStruct((24, PAD, 128), BF16),
            jax.ShapeDtypeStruct((24, PAD, 128), F32),
        ),
        in_specs=[
            pl.BlockSpec(memory_space=pltpu.SMEM),
            pl.BlockSpec(memory_space=pltpu.VMEM),
            pl.BlockSpec(memory_space=pltpu.HBM),
        ],
        out_specs=[pl.BlockSpec(memory_space=pltpu.VMEM)] * 2,
        scratch_shapes=[
            pltpu.VMEM(tokens.shape, BF16),
            pltpu.VMEM((features + 32, 128), F32),
            pltpu.SemaphoreType.DMA((BLOCKS,)),
        ],
        compiler_params=pltpu.CompilerParams(vmem_limit_bytes=60_000_000),
        name="grad",
    )(me.reshape(1), cotangent, tokens)


def apply_kernel(
    rows_dev, me_ref, mine_ref, other_ref, tokens_hbm, out_ref, tokens_ref, rows_ref, sems
):
    features = tokens_ref.shape[1]
    width = features // BLOCKS
    copies = fetch(tokens_hbm, tokens_ref, sems)
    my_a, my_b, my_x, my_c = slot_bits(me_ref)
    even = my_c == 0
    total = jnp.zeros(out_ref.shape, F32)
    chip = 0
    for i in range(BLOCKS):
        while chip < DP // NC and 2 * chip * rows_dev < (i + 1) * width:
            z, x = chip // NX, chip % NX
            steps_a = lax.rem(my_a + 3 - z // 2, 3) + jnp.where(my_b == z % 2, 0, 3)
            apart = jnp.bitwise_xor(my_x, x)
            zero, one = pick_of(apart, (0, 6, 18, 12)), pick_of(apart, (0, 12, 18, 6))
            mine = mine_ref[steps_a + jnp.where(even, zero, one)].astype(F32)
            other = other_ref[steps_a + jnp.where(even, one, zero)].astype(F32)
            start = 2 * chip * rows_dev
            rows_ref[start : start + PAD, :] = jnp.where(even, mine, other)
            start += rows_dev
            rows_ref[start : start + PAD, :] = jnp.where(even, other, mine)
            chip += 1
        block = slice(i * width, i * width + width)
        copies[i].wait()
        total += jnp.dot(
            tokens_ref[:, block], rows_ref[block, :].astype(BF16), preferred_element_type=F32
        )
    out_ref[...] = total.astype(BF16)


def apply(me, mine, other, tokens, rows_dev):
    tall, features = tokens.shape
    return pl.pallas_call(
        functools.partial(apply_kernel, rows_dev),
        out_shape=jax.ShapeDtypeStruct((tall, 128), BF16),
        in_specs=[pl.BlockSpec(memory_space=pltpu.SMEM)]
        + [pl.BlockSpec(memory_space=pltpu.VMEM)] * 2
        + [pl.BlockSpec(memory_space=pltpu.HBM)],
        scratch_shapes=[
            pltpu.VMEM(tokens.shape, BF16),
            pltpu.VMEM((features + 32, 128), F32),
            pltpu.SemaphoreType.DMA((BLOCKS,)),
        ],
        compiler_params=pltpu.CompilerParams(vmem_limit_bytes=60_000_000),
        name="apply",
    )(me.reshape(1), mine, other, tokens)


def per_device(tokens, cotangent, master, first_moment, second_moment, old_rows):
    rows_dev = master.shape[0]
    me = lax.axis_index("dp")

    send, keep = grad(me, cotangent, tokens, rows_dev)
    got = shift(send, dc=1)
    next_x = (keep[:12] + got[:12].astype(F32)).astype(BF16)

    box = route(old_rows, master, first_moment, second_moment)
    got_x = shift(next_x, dx=FIRST)
    arrived = lax.all_to_all(box, "dp", split_axis=0, concat_axis=0, tiled=True)
    weight_own, first, second = place(arrived)

    next_x = keep[12:18] + got[12:18].astype(F32) + got_x[:6].astype(F32)
    next_x = next_x.astype(BF16)
    next_x, got_x = lax.optimization_barrier((next_x, got_x))
    last_x = shift(next_x, dx=SECOND)
    sums = (
        keep[18:] + got[18:].astype(F32) + got_x[6:].astype(F32) + last_x.astype(F32)
    )
    near, far = sums[:3], sums[3:]
    got_z = shift(far.astype(BF16), db=1)
    near = near + got_z.astype(F32)
    gradient = (
        near[0]
        + shift(near[1].astype(BF16), da=1).astype(F32)
        + shift(near[2].astype(BF16), da=2).astype(F32)
    )[:rows_dev]

    squares = jnp.sum(gradient * gradient)
    high = squares.astype(BF16)
    middle = (squares - high.astype(F32)).astype(BF16)
    low = (squares - high.astype(F32) - middle.astype(F32)).astype(BF16)
    row = lax.broadcasted_iota(jnp.int32, (PAD, 128), 0)
    own = jnp.where(
        row < rows_dev,
        weight_own,
        jnp.where(row == rows_dev, high, jnp.where(row == rows_dev + 1, middle, low)),
    )

    three = jnp.stack([own, shift(own, da=1), shift(own, da=2)])
    run = jnp.concatenate([three, shift(three, db=1)], axis=0)
    pair = jnp.concatenate([run, shift(run, dx=FIRST)], axis=0)
    rest = shift(pair, dx=SECOND)

    squares = jnp.sum(pair[:, rows_dev : rows_dev + 3, :].astype(F32), axis=(0, 1)).reshape(1, 128)
    squares = squares + swap(squares, 8)
    half = lax.axis_size("tensor") // 2
    groups = [list(range(half)), list(range(half, 2 * half))]
    squares = lax.psum(squares, "tensor", axis_index_groups=groups)
    rest, squares = lax.optimization_barrier((rest, squares))
    mine = jnp.concatenate([pair, rest], axis=0)
    other = shift(mine, dc=1)
    squares = squares + shift(squares, dx=SECOND)
    last = shift(squares, dc=1)
    keys_values = apply(me, mine, other, tokens, rows_dev)
    keys_values, last = lax.optimization_barrier((keys_values, last))
    squares = (squares + last)[0, 0]

    factor = clip_norm / (jnp.sqrt(squares) + 1e-06)
    clipped = gradient * factor
    moment_one = beta_one * first[:rows_dev] + (1.0 - beta_one) * clipped
    moment_two = beta_two * second[:rows_dev] + (1.0 - beta_two) * clipped * clipped
    update = moment_one / (jnp.sqrt(moment_two) + adam_eps)
    return (keys_values, update)


def solution(mesh):
    in_specs = (
        P("dp", None),
        P("dp", "tensor"),
        P("dp", "tensor"),
        P("dp", "tensor"),
        P("dp", "tensor"),
        P("dp"),
    )
    out_specs = (P("dp", "tensor"), P("dp", "tensor"))
    return jax.shard_map(
        per_device, mesh=mesh, in_specs=in_specs, out_specs=out_specs, check_vma=False
    )
```

```python
import functools

import jax
import jax.numpy as jnp
from jax import lax
from jax.experimental import pallas as pl
from jax.experimental.pallas import tpu as pltpu
from jax.sharding import PartitionSpec as P

beta_one = 0.9
beta_two = 0.95
adam_eps = 1e-08
clip_norm = 1.0

F32, BF16 = jnp.float32, jnp.bfloat16
NZ, NX, NC = 6, 4, 2
DP = NZ * NX * NC
CAP = 8
PAD = 176
BLOCKS = 8


FIRST, SECOND = (1, 3), (3, 1)


def shift(value, dx=(0, 0), dc=0):
    pairs = []
    for z in range(NZ):
        for x in range(NX):
            for c in range(NC):
                source = (z * NX + x) * NC + c
                pairs.append((source, (z * NX + (x ^ dx[c])) * NC + (c ^ dc)))
    return lax.ppermute(value, "dp", pairs)


def along_z(value):
    rest = NX * NC
    groups = [[z * rest + i for z in range(NZ)] for i in range(rest)]
    return lax.all_to_all(
        value, "dp", split_axis=0, concat_axis=0, tiled=True, axis_index_groups=groups
    )


def iota(shape, axis):
    return lax.broadcasted_iota(jnp.int32, shape, axis).astype(F32)


def route_kernel(rows_ref, master_ref, first_ref, second_ref, out_ref):
    count = rows_ref.shape[1]
    rows_dev = float(count)
    along = rows_ref[...].astype(F32)
    line, column = iota((count, count), 0), iota((count, count), 1)
    down = jnp.sum(jnp.where(line == column, along, 0.0), axis=1, keepdims=True)
    owner_down = jnp.sum(
        jnp.where(down >= rows_dev * (iota((count, 128), 1) + 1.0), 1.0, 0.0), axis=1, keepdims=True
    )
    owner_along = jnp.sum(
        jnp.where(along >= rows_dev * (iota((DP, count), 0) + 1.0), 1.0, 0.0), axis=0, keepdims=True
    )
    before = jnp.where((owner_down == owner_along) & (line < column), 1.0, 0.0)
    within = jnp.sum(before, axis=0, keepdims=True)
    code = owner_along * CAP + within
    pick = jnp.where(code == iota((DP * CAP, count), 0), 1.0, 0.0).astype(BF16)
    label = jnp.broadcast_to(down - rows_dev * owner_down + 1.0, (count, 128))
    data = jnp.concatenate(
        [master_ref[...], first_ref[...], second_ref[...], label], axis=1
    ).astype(BF16)
    sent = jnp.dot(pick, data, preferred_element_type=F32)
    parts = [sent[:, 128 * k : 128 * k + 128].reshape(DP, CAP, 128) for k in range(4)]
    out_ref[...] = jnp.concatenate(parts, axis=1).astype(BF16)


def route(rows, master, first, second):
    return pl.pallas_call(
        route_kernel,
        out_shape=jax.ShapeDtypeStruct((DP, 4 * CAP, 128), BF16),
        name="route",
    )(rows.reshape(1, -1), master, first, second)


def place_kernel(box_ref, weight_ref, first_ref, second_ref):
    box = box_ref[...].astype(F32)
    parts = [box[:, CAP * k : CAP * k + CAP, :].reshape(DP * CAP, 128) for k in range(4)]
    label = parts[3]
    lane = iota((DP * CAP, 128), 1)
    pick = jnp.concatenate(
        [jnp.where(label == lane + 1.0, 1.0, 0.0), jnp.where(label == lane + 129.0, 1.0, 0.0)],
        axis=1,
    ).astype(BF16)
    data = jnp.concatenate(parts[:3], axis=1).astype(BF16)
    placed = lax.dot_general(
        pick, data, (((0,), (0,)), ((), ())), preferred_element_type=F32
    )
    weight_ref[...] = placed[:PAD, :128].astype(BF16)
    first_ref[...] = placed[:PAD, 128:256]
    second_ref[...] = placed[:PAD, 256:384]


def place(box):
    return pl.pallas_call(
        place_kernel,
        out_shape=(
            jax.ShapeDtypeStruct((PAD, 128), BF16),
            jax.ShapeDtypeStruct((PAD, 128), F32),
            jax.ShapeDtypeStruct((PAD, 128), F32),
        ),
        name="place",
    )(box)


def pick_of(key, values):
    chosen = jnp.int32(values[-1])
    for index, value in enumerate(values[:-1]):
        chosen = jnp.where(key == index, jnp.int32(value), chosen)
    return chosen


def fetch(tokens_hbm, tokens_ref, sems):
    width = tokens_ref.shape[1] // BLOCKS
    copies = [
        pltpu.make_async_copy(
            tokens_hbm.at[:, pl.ds(i * width, width)],
            tokens_ref.at[:, pl.ds(i * width, width)],
            sems.at[i],
        )
        for i in range(BLOCKS)
    ]
    for copy in copies:
        copy.start()
    return copies


def grad_kernel(
    rows_dev, me_ref, cot_ref, tokens_hbm, send_ref, keep_ref, tokens_ref, whole_ref, sems
):
    features = tokens_ref.shape[1]
    width = features // BLOCKS
    copies = fetch(tokens_hbm, tokens_ref, sems)
    my_x, even = lax.rem(lax.div(me_ref[0], NC), NX), lax.rem(me_ref[0], NC) == 0
    whole_ref[features:, :] = jnp.zeros((whole_ref.shape[0] - features, 128), F32)
    turned = cot_ref[...].T
    chip = 0
    for i in range(BLOCKS):
        copies[i].wait()
        across = jnp.dot(
            turned, tokens_ref[:, i * width : i * width + width], preferred_element_type=F32
        )
        whole_ref[i * width : i * width + width, :] = across.T
        ready = (i + 1) * width if i < BLOCKS - 1 else whole_ref.shape[0]
        while chip < DP // NC and (2 * chip + 1) * rows_dev + PAD <= ready:
            z, x = chip // NX, chip % NX
            apart = jnp.bitwise_xor(my_x, x)
            zero, one = pick_of(apart, (18, 6, 0, 12)), pick_of(apart, (18, 12, 0, 6))
            kept = z + jnp.where(even, zero, one)
            sent = z + jnp.where(even, one, zero)
            first = whole_ref[2 * chip * rows_dev : 2 * chip * rows_dev + PAD, :]
            second = whole_ref[(2 * chip + 1) * rows_dev : (2 * chip + 1) * rows_dev + PAD, :]
            keep_ref[kept] = jnp.where(even, first, second)
            send_ref[sent] = jnp.where(even, second, first).astype(BF16)
            chip += 1


def grad(me, cotangent, tokens, rows_dev):
    _, features = tokens.shape
    return pl.pallas_call(
        functools.partial(grad_kernel, rows_dev),
        out_shape=(
            jax.ShapeDtypeStruct((24, PAD, 128), BF16),
            jax.ShapeDtypeStruct((24, PAD, 128), F32),
        ),
        in_specs=[
            pl.BlockSpec(memory_space=pltpu.SMEM),
            pl.BlockSpec(memory_space=pltpu.VMEM),
            pl.BlockSpec(memory_space=pltpu.HBM),
        ],
        out_specs=[pl.BlockSpec(memory_space=pltpu.VMEM)] * 2,
        scratch_shapes=[
            pltpu.VMEM(tokens.shape, BF16),
            pltpu.VMEM((features + 32, 128), F32),
            pltpu.SemaphoreType.DMA((BLOCKS,)),
        ],
        compiler_params=pltpu.CompilerParams(vmem_limit_bytes=60_000_000),
        name="grad",
    )(me.reshape(1), cotangent, tokens)


def apply_kernel(
    rows_dev, me_ref, mine_ref, other_ref, tokens_hbm, out_ref, tokens_ref, rows_ref, sems
):
    features = tokens_ref.shape[1]
    width = features // BLOCKS
    copies = fetch(tokens_hbm, tokens_ref, sems)
    my_x, even = lax.rem(lax.div(me_ref[0], NC), NX), lax.rem(me_ref[0], NC) == 0
    total = jnp.zeros(out_ref.shape, F32)
    chip = 0
    for i in range(BLOCKS):
        while chip < DP // NC and 2 * chip * rows_dev < (i + 1) * width:
            z, x = chip // NX, chip % NX
            apart = jnp.bitwise_xor(my_x, x)
            zero, one = pick_of(apart, (0, 6, 18, 12)), pick_of(apart, (0, 12, 18, 6))
            mine = mine_ref[z + jnp.where(even, zero, one)].astype(F32)
            other = other_ref[z + jnp.where(even, one, zero)].astype(F32)
            start = 2 * chip * rows_dev
            rows_ref[start : start + PAD, :] = jnp.where(even, mine, other)
            start += rows_dev
            rows_ref[start : start + PAD, :] = jnp.where(even, other, mine)
            chip += 1
        block = slice(i * width, i * width + width)
        copies[i].wait()
        total += jnp.dot(
            tokens_ref[:, block], rows_ref[block, :].astype(BF16), preferred_element_type=F32
        )
    out_ref[...] = total.astype(BF16)


def apply(me, mine, other, tokens, rows_dev):
    tall, features = tokens.shape
    return pl.pallas_call(
        functools.partial(apply_kernel, rows_dev),
        out_shape=jax.ShapeDtypeStruct((tall, 128), BF16),
        in_specs=[pl.BlockSpec(memory_space=pltpu.SMEM)]
        + [pl.BlockSpec(memory_space=pltpu.VMEM)] * 2
        + [pl.BlockSpec(memory_space=pltpu.HBM)],
        scratch_shapes=[
            pltpu.VMEM(tokens.shape, BF16),
            pltpu.VMEM((features + 32, 128), F32),
            pltpu.SemaphoreType.DMA((BLOCKS,)),
        ],
        compiler_params=pltpu.CompilerParams(vmem_limit_bytes=60_000_000),
        name="apply",
    )(me.reshape(1), mine, other, tokens)


def per_device(tokens, cotangent, master, first_moment, second_moment, old_rows):
    rows_dev = master.shape[0]
    me = lax.axis_index("dp")

    send, keep = grad(me, cotangent, tokens, rows_dev)
    got = shift(send, dc=1)
    next_x = (keep[:12] + got[:12].astype(F32)).astype(BF16)

    box = route(old_rows, master, first_moment, second_moment)
    got_x = shift(next_x, dx=FIRST)
    arrived = lax.all_to_all(box, "dp", split_axis=0, concat_axis=0, tiled=True)
    weight_own, first, second = place(arrived)

    next_x = keep[12:18] + got[12:18].astype(F32) + got_x[:6].astype(F32)
    next_x = next_x.astype(BF16)
    next_x, got_x = lax.optimization_barrier((next_x, got_x))
    last_x = shift(next_x, dx=SECOND)
    sums = (
        keep[18:] + got[18:].astype(F32) + got_x[6:].astype(F32) + last_x.astype(F32)
    )
    got_z = along_z(sums.astype(BF16))
    gradient = jnp.sum(got_z.astype(F32), axis=0)[:rows_dev]

    squares = jnp.sum(gradient * gradient)
    high = squares.astype(BF16)
    middle = (squares - high.astype(F32)).astype(BF16)
    low = (squares - high.astype(F32) - middle.astype(F32)).astype(BF16)
    row = lax.broadcasted_iota(jnp.int32, (PAD, 128), 0)
    own = jnp.where(
        row < rows_dev,
        weight_own,
        jnp.where(row == rows_dev, high, jnp.where(row == rows_dev + 1, middle, low)),
    )

    run = along_z(jnp.broadcast_to(own, (NZ, PAD, 128)))
    pair = jnp.concatenate([run, shift(run, dx=FIRST)], axis=0)
    mine = jnp.concatenate([pair, shift(pair, dx=SECOND)], axis=0)
    other = shift(mine, dc=1)

    ends = slice(rows_dev, rows_dev + 3)
    squares = jnp.sum(mine[:, ends, :].astype(F32) + other[:, ends, :].astype(F32), axis=(0, 1))
    copies = jnp.broadcast_to(squares, (lax.axis_size("tensor"), 8, 128))
    parts = lax.all_to_all(copies, "tensor", split_axis=0, concat_axis=0, tiled=True)
    keys_values = apply(me, mine, other, tokens, rows_dev)
    keys_values, parts = lax.optimization_barrier((keys_values, parts))
    squares = jnp.sum(parts[:, 0, 0])

    factor = clip_norm / (jnp.sqrt(squares) + 1e-06)
    clipped = gradient * factor
    moment_one = beta_one * first[:rows_dev] + (1.0 - beta_one) * clipped
    moment_two = beta_two * second[:rows_dev] + (1.0 - beta_two) * clipped * clipped
    update = moment_one / (jnp.sqrt(moment_two) + adam_eps)
    return (keys_values, update)


def solution(mesh):
    in_specs = (
        P("dp", None),
        P("dp", "tensor"),
        P("dp", "tensor"),
        P("dp", "tensor"),
        P("dp", "tensor"),
        P("dp"),
    )
    out_specs = (P("dp", "tensor"), P("dp", "tensor"))
    return jax.shard_map(
        per_device, mesh=mesh, in_specs=in_specs, out_specs=out_specs, check_vma=False
    )
```

```python
import functools

import jax
import jax.numpy as jnp
from jax import lax
from jax.experimental import pallas as pl
from jax.experimental.pallas import tpu as pltpu
from jax.sharding import PartitionSpec as P

beta_one = 0.9
beta_two = 0.95
adam_eps = 1e-08
clip_norm = 1.0

F32, BF16 = jnp.float32, jnp.bfloat16
NZ, NX, NC = 6, 4, 2
DP = NZ * NX * NC
CAP = 8
PAD = 176
BLOCKS = 8


FIRST, SECOND = (1, 3), (3, 1)


def shift(value, dx=(0, 0), dc=0):
    pairs = []
    for z in range(NZ):
        for x in range(NX):
            for c in range(NC):
                source = (z * NX + x) * NC + c
                pairs.append((source, (z * NX + (x ^ dx[c])) * NC + (c ^ dc)))
    return lax.ppermute(value, "dp", pairs)


def along_z(value):
    rest = NX * NC
    groups = [[z * rest + i for z in range(NZ)] for i in range(rest)]
    return lax.all_to_all(
        value, "dp", split_axis=0, concat_axis=0, tiled=True, axis_index_groups=groups
    )


def sum_over(value, axis):
    copies = jnp.broadcast_to(value, (lax.axis_size(axis), 8, 128))
    parts = lax.all_to_all(copies, axis, split_axis=0, concat_axis=0, tiled=True)
    return jnp.sum(parts[:, 0, 0])


def iota(shape, axis):
    return lax.broadcasted_iota(jnp.int32, shape, axis).astype(F32)


def route_kernel(rows_ref, master_ref, first_ref, second_ref, out_ref):
    count = rows_ref.shape[1]
    rows_dev = float(count)
    along = rows_ref[...].astype(F32)
    line, column = iota((count, count), 0), iota((count, count), 1)
    down = jnp.sum(jnp.where(line == column, along, 0.0), axis=1, keepdims=True)
    owner_down = jnp.sum(
        jnp.where(down >= rows_dev * (iota((count, 128), 1) + 1.0), 1.0, 0.0), axis=1, keepdims=True
    )
    owner_along = jnp.sum(
        jnp.where(along >= rows_dev * (iota((DP, count), 0) + 1.0), 1.0, 0.0), axis=0, keepdims=True
    )
    before = jnp.where((owner_down == owner_along) & (line < column), 1.0, 0.0)
    within = jnp.sum(before, axis=0, keepdims=True)
    code = owner_along * CAP + within
    pick = jnp.where(code == iota((DP * CAP, count), 0), 1.0, 0.0).astype(BF16)
    label = jnp.broadcast_to(down - rows_dev * owner_down + 1.0, (count, 128))
    data = jnp.concatenate(
        [master_ref[...], first_ref[...], second_ref[...], label], axis=1
    ).astype(BF16)
    sent = jnp.dot(pick, data, preferred_element_type=F32)
    parts = [sent[:, 128 * k : 128 * k + 128].reshape(DP, CAP, 128) for k in range(4)]
    out_ref[...] = jnp.concatenate(parts, axis=1).astype(BF16)


def route(rows, master, first, second):
    return pl.pallas_call(
        route_kernel,
        out_shape=jax.ShapeDtypeStruct((DP, 4 * CAP, 128), BF16),
        name="route",
    )(rows.reshape(1, -1), master, first, second)


def place_kernel(box_ref, weight_ref, first_ref, second_ref):
    box = box_ref[...].astype(F32)
    parts = [box[:, CAP * k : CAP * k + CAP, :].reshape(DP * CAP, 128) for k in range(4)]
    label = parts[3]
    lane = iota((DP * CAP, 128), 1)
    pick = jnp.concatenate(
        [jnp.where(label == lane + 1.0, 1.0, 0.0), jnp.where(label == lane + 129.0, 1.0, 0.0)],
        axis=1,
    ).astype(BF16)
    data = jnp.concatenate(parts[:3], axis=1).astype(BF16)
    placed = lax.dot_general(
        pick, data, (((0,), (0,)), ((), ())), preferred_element_type=F32
    )
    weight = placed[:PAD, :128].astype(BF16)
    for z in range(NZ):
        weight_ref[z] = weight
    first_ref[...] = placed[:PAD, 128:256]
    second_ref[...] = placed[:PAD, 256:384]


def place(box):
    return pl.pallas_call(
        place_kernel,
        out_shape=(
            jax.ShapeDtypeStruct((NZ, PAD, 128), BF16),
            jax.ShapeDtypeStruct((PAD, 128), F32),
            jax.ShapeDtypeStruct((PAD, 128), F32),
        ),
        name="place",
    )(box)


def pick_of(key, values):
    chosen = jnp.int32(values[-1])
    for index, value in enumerate(values[:-1]):
        chosen = jnp.where(key == index, jnp.int32(value), chosen)
    return chosen


def fetch(tokens_hbm, tokens_ref, sems):
    width = tokens_ref.shape[1] // BLOCKS
    copies = [
        pltpu.make_async_copy(
            tokens_hbm.at[:, pl.ds(i * width, width)],
            tokens_ref.at[:, pl.ds(i * width, width)],
            sems.at[i],
        )
        for i in range(BLOCKS)
    ]
    for copy in copies:
        copy.start()
    return copies


def grad_kernel(
    rows_dev, me_ref, cot_ref, tokens_hbm, send_ref, keep_ref, tokens_ref, whole_ref, sems
):
    features = tokens_ref.shape[1]
    width = features // BLOCKS
    copies = fetch(tokens_hbm, tokens_ref, sems)
    my_x, even = lax.rem(lax.div(me_ref[0], NC), NX), lax.rem(me_ref[0], NC) == 0
    whole_ref[features:, :] = jnp.zeros((whole_ref.shape[0] - features, 128), F32)
    turned = cot_ref[...].T
    chip = 0
    for i in range(BLOCKS):
        copies[i].wait()
        across = jnp.dot(
            turned, tokens_ref[:, i * width : i * width + width], preferred_element_type=F32
        )
        whole_ref[i * width : i * width + width, :] = across.T
        ready = (i + 1) * width if i < BLOCKS - 1 else whole_ref.shape[0]
        while chip < DP // NC and (2 * chip + 1) * rows_dev + PAD <= ready:
            z, x = chip // NX, chip % NX
            apart = jnp.bitwise_xor(my_x, x)
            zero, one = pick_of(apart, (18, 6, 0, 12)), pick_of(apart, (18, 12, 0, 6))
            kept = z + jnp.where(even, zero, one)
            sent = z + jnp.where(even, one, zero)
            first = whole_ref[2 * chip * rows_dev : 2 * chip * rows_dev + PAD, :]
            second = whole_ref[(2 * chip + 1) * rows_dev : (2 * chip + 1) * rows_dev + PAD, :]
            keep_ref[kept] = jnp.where(even, first, second)
            send_ref[sent] = jnp.where(even, second, first).astype(BF16)
            chip += 1


def grad(me, cotangent, tokens, rows_dev):
    _, features = tokens.shape
    return pl.pallas_call(
        functools.partial(grad_kernel, rows_dev),
        out_shape=(
            jax.ShapeDtypeStruct((24, PAD, 128), BF16),
            jax.ShapeDtypeStruct((24, PAD, 128), F32),
        ),
        in_specs=[
            pl.BlockSpec(memory_space=pltpu.SMEM),
            pl.BlockSpec(memory_space=pltpu.VMEM),
            pl.BlockSpec(memory_space=pltpu.HBM),
        ],
        out_specs=[pl.BlockSpec(memory_space=pltpu.VMEM)] * 2,
        scratch_shapes=[
            pltpu.VMEM(tokens.shape, BF16),
            pltpu.VMEM((features + 32, 128), F32),
            pltpu.SemaphoreType.DMA((BLOCKS,)),
        ],
        compiler_params=pltpu.CompilerParams(vmem_limit_bytes=60_000_000),
        name="grad",
    )(me.reshape(1), cotangent, tokens)


def apply_kernel(
    rows_dev, me_ref, mine_ref, other_ref, tokens_hbm, out_ref, tokens_ref, rows_ref, sems
):
    features = tokens_ref.shape[1]
    width = features // BLOCKS
    copies = fetch(tokens_hbm, tokens_ref, sems)
    my_x, even = lax.rem(lax.div(me_ref[0], NC), NX), lax.rem(me_ref[0], NC) == 0
    total = jnp.zeros(out_ref.shape, F32)
    chip = 0
    for i in range(BLOCKS):
        while chip < DP // NC and 2 * chip * rows_dev < (i + 1) * width:
            z, x = chip // NX, chip % NX
            apart = jnp.bitwise_xor(my_x, x)
            zero, one = pick_of(apart, (0, 6, 18, 12)), pick_of(apart, (0, 12, 18, 6))
            mine = mine_ref[z + jnp.where(even, zero, one)].astype(F32)
            other = other_ref[z + jnp.where(even, one, zero)].astype(F32)
            start = 2 * chip * rows_dev
            rows_ref[start : start + PAD, :] = jnp.where(even, mine, other)
            start += rows_dev
            rows_ref[start : start + PAD, :] = jnp.where(even, other, mine)
            chip += 1
        block = slice(i * width, i * width + width)
        copies[i].wait()
        total += jnp.dot(
            tokens_ref[:, block], rows_ref[block, :].astype(BF16), preferred_element_type=F32
        )
    out_ref[...] = total.astype(BF16)


def apply(me, mine, other, tokens, rows_dev):
    tall, features = tokens.shape
    return pl.pallas_call(
        functools.partial(apply_kernel, rows_dev),
        out_shape=jax.ShapeDtypeStruct((tall, 128), BF16),
        in_specs=[pl.BlockSpec(memory_space=pltpu.SMEM)]
        + [pl.BlockSpec(memory_space=pltpu.VMEM)] * 2
        + [pl.BlockSpec(memory_space=pltpu.HBM)],
        scratch_shapes=[
            pltpu.VMEM(tokens.shape, BF16),
            pltpu.VMEM((features + 32, 128), F32),
            pltpu.SemaphoreType.DMA((BLOCKS,)),
        ],
        compiler_params=pltpu.CompilerParams(vmem_limit_bytes=60_000_000),
        name="apply",
    )(me.reshape(1), mine, other, tokens)


def per_device(tokens, cotangent, master, first_moment, second_moment, old_rows):
    rows_dev = master.shape[0]
    me = lax.axis_index("dp")

    box = route(old_rows, master, first_moment, second_moment)
    arrived = lax.all_to_all(box, "dp", split_axis=0, concat_axis=0, tiled=True)
    weight_own, first, second = place(arrived)

    send, keep = grad(me, cotangent, tokens, rows_dev)
    got = shift(send, dc=1)
    next_x = (keep[:12] + got[:12].astype(F32)).astype(BF16)
    got_x = shift(next_x, dx=FIRST)
    next_x = keep[12:18] + got[12:18].astype(F32) + got_x[:6].astype(F32)
    next_x = next_x.astype(BF16)
    next_x, got_x = lax.optimization_barrier((next_x, got_x))
    last_x = shift(next_x, dx=SECOND)
    sums = keep[18:] + got[18:].astype(F32) + got_x[6:].astype(F32) + last_x.astype(F32)
    got_z = along_z(sums.astype(BF16))
    gradient = jnp.sum(got_z.astype(F32), axis=0)[:rows_dev]

    run = along_z(weight_own)
    west = shift(run, dx=FIRST)
    pair = jnp.concatenate([run, west], axis=0)
    rest = shift(pair, dx=SECOND)
    mine = jnp.concatenate([pair, rest], axis=0)
    other = shift(mine, dc=1)

    squares = jnp.sum(gradient * gradient)
    squares = sum_over(squares, "tensor")
    squares = sum_over(squares, "dp")
    keys_values = apply(me, mine, other, tokens, rows_dev)

    factor = clip_norm / (jnp.sqrt(squares) + 1e-06)
    clipped = gradient * factor
    moment_one = beta_one * first[:rows_dev] + (1.0 - beta_one) * clipped
    moment_two = beta_two * second[:rows_dev] + (1.0 - beta_two) * clipped * clipped
    update = moment_one / (jnp.sqrt(moment_two) + adam_eps)
    return (keys_values, update)


def solution(mesh):
    in_specs = (
        P("dp", None),
        P("dp", "tensor"),
        P("dp", "tensor"),
        P("dp", "tensor"),
        P("dp", "tensor"),
        P("dp"),
    )
    out_specs = (P("dp", "tensor"), P("dp", "tensor"))
    return jax.shard_map(
        per_device, mesh=mesh, in_specs=in_specs, out_specs=out_specs, check_vma=False
    )
```

```python
import functools

import jax
import jax.numpy as jnp
from jax import lax
from jax.experimental import pallas as pl
from jax.experimental.pallas import tpu as pltpu
from jax.sharding import PartitionSpec as P

beta_one = 0.9
beta_two = 0.95
adam_eps = 1e-08
clip_norm = 1.0

F32, BF16 = jnp.float32, jnp.bfloat16
NZ, NX, NC = 6, 4, 2
DP = NZ * NX * NC
CAP = 8
PAD = 176
BLOCKS = 8


FIRST, SECOND = (1, 3), (3, 1)


def shift(value, dx=(0, 0), dc=0):
    pairs = []
    for z in range(NZ):
        for x in range(NX):
            for c in range(NC):
                source = (z * NX + x) * NC + c
                pairs.append((source, (z * NX + (x ^ dx[c])) * NC + (c ^ dc)))
    return lax.ppermute(value, "dp", pairs)


def along_z(value):
    rest = NX * NC
    groups = [[z * rest + i for z in range(NZ)] for i in range(rest)]
    return lax.all_to_all(
        value, "dp", split_axis=0, concat_axis=0, tiled=True, axis_index_groups=groups
    )


def exchange(copies, axis):
    return lax.all_to_all(copies, axis, split_axis=0, concat_axis=0, tiled=True)


def iota(shape, axis):
    return lax.broadcasted_iota(jnp.int32, shape, axis).astype(F32)


def route_kernel(rows_ref, master_ref, first_ref, second_ref, out_ref):
    count = rows_ref.shape[1]
    rows_dev = float(count)
    along = rows_ref[...].astype(F32)
    line, column = iota((count, count), 0), iota((count, count), 1)
    down = jnp.sum(jnp.where(line == column, along, 0.0), axis=1, keepdims=True)
    owner_down = jnp.sum(
        jnp.where(down >= rows_dev * (iota((count, 128), 1) + 1.0), 1.0, 0.0), axis=1, keepdims=True
    )
    owner_along = jnp.sum(
        jnp.where(along >= rows_dev * (iota((DP, count), 0) + 1.0), 1.0, 0.0), axis=0, keepdims=True
    )
    before = jnp.where((owner_down == owner_along) & (line < column), 1.0, 0.0)
    within = jnp.sum(before, axis=0, keepdims=True)
    code = owner_along * CAP + within
    pick = jnp.where(code == iota((DP * CAP, count), 0), 1.0, 0.0).astype(BF16)
    label = jnp.broadcast_to(down - rows_dev * owner_down + 1.0, (count, 128))
    data = jnp.concatenate(
        [master_ref[...], first_ref[...], second_ref[...], label], axis=1
    ).astype(BF16)
    sent = jnp.dot(pick, data, preferred_element_type=F32)
    parts = [sent[:, 128 * k : 128 * k + 128].reshape(DP, CAP, 128) for k in range(4)]
    out_ref[...] = jnp.concatenate(parts, axis=1).astype(BF16)


def route(rows, master, first, second):
    return pl.pallas_call(
        route_kernel,
        out_shape=jax.ShapeDtypeStruct((DP, 4 * CAP, 128), BF16),
        name="route",
    )(rows.reshape(1, -1), master, first, second)


def place_kernel(box_ref, weight_ref, first_ref, second_ref):
    box = box_ref[...].astype(F32)
    parts = [box[:, CAP * k : CAP * k + CAP, :].reshape(DP * CAP, 128) for k in range(4)]
    label = parts[3]
    lane = iota((DP * CAP, 128), 1)
    pick = jnp.concatenate(
        [jnp.where(label == lane + 1.0, 1.0, 0.0), jnp.where(label == lane + 129.0, 1.0, 0.0)],
        axis=1,
    ).astype(BF16)
    data = jnp.concatenate(parts[:3], axis=1).astype(BF16)
    placed = lax.dot_general(
        pick, data, (((0,), (0,)), ((), ())), preferred_element_type=F32
    )
    weight = placed[:PAD, :128].astype(BF16)
    for z in range(NZ):
        weight_ref[z] = weight
    first_ref[...] = placed[:PAD, 128:256]
    second_ref[...] = placed[:PAD, 256:384]


def place(box):
    return pl.pallas_call(
        place_kernel,
        out_shape=(
            jax.ShapeDtypeStruct((NZ, PAD, 128), BF16),
            jax.ShapeDtypeStruct((PAD, 128), F32),
            jax.ShapeDtypeStruct((PAD, 128), F32),
        ),
        name="place",
    )(box)


def pick_of(key, values):
    chosen = jnp.int32(values[-1])
    for index, value in enumerate(values[:-1]):
        chosen = jnp.where(key == index, jnp.int32(value), chosen)
    return chosen


def fetch(tokens_hbm, tokens_ref, sems):
    width = tokens_ref.shape[1] // BLOCKS
    copies = [
        pltpu.make_async_copy(
            tokens_hbm.at[:, pl.ds(i * width, width)],
            tokens_ref.at[:, pl.ds(i * width, width)],
            sems.at[i],
        )
        for i in range(BLOCKS)
    ]
    for copy in copies:
        copy.start()
    return copies


def grad_kernel(
    rows_dev, me_ref, cot_ref, tokens_hbm, send_ref, keep_ref, tokens_ref, whole_ref, sems
):
    features = tokens_ref.shape[1]
    width = features // BLOCKS
    copies = fetch(tokens_hbm, tokens_ref, sems)
    my_x, even = lax.rem(lax.div(me_ref[0], NC), NX), lax.rem(me_ref[0], NC) == 0
    whole_ref[features:, :] = jnp.zeros((whole_ref.shape[0] - features, 128), F32)
    turned = cot_ref[...].T
    chip = 0
    for i in range(BLOCKS):
        copies[i].wait()
        across = jnp.dot(
            turned, tokens_ref[:, i * width : i * width + width], preferred_element_type=F32
        )
        whole_ref[i * width : i * width + width, :] = across.T
        ready = (i + 1) * width if i < BLOCKS - 1 else whole_ref.shape[0]
        while chip < DP // NC and (2 * chip + 1) * rows_dev + PAD <= ready:
            z, x = chip // NX, chip % NX
            apart = jnp.bitwise_xor(my_x, x)
            zero, one = pick_of(apart, (18, 6, 0, 12)), pick_of(apart, (18, 12, 0, 6))
            kept = z + jnp.where(even, zero, one)
            sent = z + jnp.where(even, one, zero)
            first = whole_ref[2 * chip * rows_dev : 2 * chip * rows_dev + PAD, :]
            second = whole_ref[(2 * chip + 1) * rows_dev : (2 * chip + 1) * rows_dev + PAD, :]
            keep_ref[kept] = jnp.where(even, first, second)
            send_ref[sent] = jnp.where(even, second, first).astype(BF16)
            chip += 1


def grad(me, cotangent, tokens, rows_dev):
    _, features = tokens.shape
    return pl.pallas_call(
        functools.partial(grad_kernel, rows_dev),
        out_shape=(
            jax.ShapeDtypeStruct((24, PAD, 128), BF16),
            jax.ShapeDtypeStruct((24, PAD, 128), F32),
        ),
        in_specs=[
            pl.BlockSpec(memory_space=pltpu.SMEM),
            pl.BlockSpec(memory_space=pltpu.VMEM),
            pl.BlockSpec(memory_space=pltpu.HBM),
        ],
        out_specs=[pl.BlockSpec(memory_space=pltpu.VMEM)] * 2,
        scratch_shapes=[
            pltpu.VMEM(tokens.shape, BF16),
            pltpu.VMEM((features + 32, 128), F32),
            pltpu.SemaphoreType.DMA((BLOCKS,)),
        ],
        compiler_params=pltpu.CompilerParams(vmem_limit_bytes=60_000_000),
        name="grad",
    )(me.reshape(1), cotangent, tokens)


def apply_kernel(
    rows_dev, me_ref, mine_ref, other_ref, tokens_hbm, out_ref, tokens_ref, rows_ref, sems
):
    features = tokens_ref.shape[1]
    width = features // BLOCKS
    copies = fetch(tokens_hbm, tokens_ref, sems)
    my_x, even = lax.rem(lax.div(me_ref[0], NC), NX), lax.rem(me_ref[0], NC) == 0
    total = jnp.zeros(out_ref.shape, F32)
    chip = 0
    for i in range(BLOCKS):
        while chip < DP // NC and 2 * chip * rows_dev < (i + 1) * width:
            z, x = chip // NX, chip % NX
            apart = jnp.bitwise_xor(my_x, x)
            zero, one = pick_of(apart, (0, 6, 18, 12)), pick_of(apart, (0, 12, 18, 6))
            mine = mine_ref[z + jnp.where(even, zero, one)].astype(F32)
            other = other_ref[z + jnp.where(even, one, zero)].astype(F32)
            start = 2 * chip * rows_dev
            rows_ref[start : start + PAD, :] = jnp.where(even, mine, other)
            start += rows_dev
            rows_ref[start : start + PAD, :] = jnp.where(even, other, mine)
            chip += 1
        block = slice(i * width, i * width + width)
        copies[i].wait()
        total += jnp.dot(
            tokens_ref[:, block], rows_ref[block, :].astype(BF16), preferred_element_type=F32
        )
    out_ref[...] = total.astype(BF16)


def apply(me, mine, other, tokens, rows_dev):
    tall, features = tokens.shape
    return pl.pallas_call(
        functools.partial(apply_kernel, rows_dev),
        out_shape=jax.ShapeDtypeStruct((tall, 128), BF16),
        in_specs=[pl.BlockSpec(memory_space=pltpu.SMEM)]
        + [pl.BlockSpec(memory_space=pltpu.VMEM)] * 2
        + [pl.BlockSpec(memory_space=pltpu.HBM)],
        scratch_shapes=[
            pltpu.VMEM(tokens.shape, BF16),
            pltpu.VMEM((features + 32, 128), F32),
            pltpu.SemaphoreType.DMA((BLOCKS,)),
        ],
        compiler_params=pltpu.CompilerParams(vmem_limit_bytes=60_000_000),
        name="apply",
    )(me.reshape(1), mine, other, tokens)


def squares_kernel(rows_dev, parts_ref, gradient_ref, copies_ref):
    gradient = jnp.sum(parts_ref[...].astype(F32), axis=0)
    gradient_ref[...] = gradient
    held = jnp.where(iota(gradient.shape, 0) < float(rows_dev), gradient, 0.0)
    tiles = (held * held).reshape(PAD // 8, 8, 128)
    copies_ref[...] = jnp.broadcast_to(jnp.sum(tiles, axis=0), copies_ref.shape)


def squares_of(parts, rows_dev, count):
    return pl.pallas_call(
        functools.partial(squares_kernel, rows_dev),
        out_shape=(
            jax.ShapeDtypeStruct((PAD, 128), F32),
            jax.ShapeDtypeStruct((count, 8, 128), F32),
        ),
        name="squares",
    )(parts)


def spread_kernel(parts_ref, copies_ref):
    copies_ref[...] = jnp.broadcast_to(jnp.sum(parts_ref[...], axis=0), copies_ref.shape)


def spread(parts, count):
    return pl.pallas_call(
        spread_kernel,
        out_shape=jax.ShapeDtypeStruct((count, 8, 128), F32),
        name="spread",
    )(parts)


def update_kernel(parts_ref, gradient_ref, first_ref, second_ref, out_ref):
    tile = jnp.sum(parts_ref[...], axis=0)
    squares = jnp.sum(jnp.sum(tile, axis=0, keepdims=True), axis=1, keepdims=True)
    factor = clip_norm / (jnp.sqrt(squares) + 1e-06)
    rows = out_ref.shape[0]
    clipped = gradient_ref[...] * factor
    moment_one = beta_one * first_ref[...] + (1.0 - beta_one) * clipped
    moment_two = beta_two * second_ref[...] + (1.0 - beta_two) * clipped * clipped
    out_ref[...] = (moment_one / (jnp.sqrt(moment_two) + adam_eps))[:rows]


def update_of(parts, gradient, first, second, rows_dev):
    return pl.pallas_call(
        update_kernel,
        out_shape=jax.ShapeDtypeStruct((rows_dev, 128), F32),
        name="update",
    )(parts, gradient, first, second)


def per_device(tokens, cotangent, master, first_moment, second_moment, old_rows):
    rows_dev = master.shape[0]
    me = lax.axis_index("dp")

    box = route(old_rows, master, first_moment, second_moment)
    arrived = lax.all_to_all(box, "dp", split_axis=0, concat_axis=0, tiled=True)
    weight_own, first, second = place(arrived)

    send, keep = grad(me, cotangent, tokens, rows_dev)
    got = shift(send, dc=1)
    next_x = (keep[:12] + got[:12].astype(F32)).astype(BF16)
    got_x = shift(next_x, dx=FIRST)
    next_x = keep[12:18] + got[12:18].astype(F32) + got_x[:6].astype(F32)
    next_x = next_x.astype(BF16)
    next_x, got_x = lax.optimization_barrier((next_x, got_x))
    last_x = shift(next_x, dx=SECOND)
    sums = keep[18:] + got[18:].astype(F32) + got_x[6:].astype(F32) + last_x.astype(F32)
    sums = sums.astype(BF16)
    got_z = along_z(sums)
    gradient, copies = squares_of(got_z, rows_dev, lax.axis_size("tensor"))

    run = along_z(weight_own)
    west = shift(run, dx=FIRST)
    pair = jnp.concatenate([run, west], axis=0)
    rest = shift(pair, dx=SECOND)
    mine = jnp.concatenate([pair, rest], axis=0)
    other = shift(mine, dc=1)

    parts = exchange(copies, "tensor")
    copies = spread(parts, DP)
    parts = exchange(copies, "dp")
    keys_values = apply(me, mine, other, tokens, rows_dev)

    update = update_of(parts, gradient, first, second, rows_dev)
    return (keys_values, update)


def solution(mesh):
    in_specs = (
        P("dp", None),
        P("dp", "tensor"),
        P("dp", "tensor"),
        P("dp", "tensor"),
        P("dp", "tensor"),
        P("dp"),
    )
    out_specs = (P("dp", "tensor"), P("dp", "tensor"))
    return jax.shard_map(
        per_device, mesh=mesh, in_specs=in_specs, out_specs=out_specs, check_vma=False
    )
```

```python
import functools

import jax
import jax.numpy as jnp
from jax import lax
from jax.experimental import pallas as pl
from jax.experimental.pallas import tpu as pltpu
from jax.sharding import PartitionSpec as P

beta_one = 0.9
beta_two = 0.95
adam_eps = 1e-08
clip_norm = 1.0

F32, BF16 = jnp.float32, jnp.bfloat16
NZ, NX, NC = 6, 4, 2
DP = NZ * NX * NC
CAP = 8
PAD = 176
BLOCKS = 8


FIRST, SECOND = (1, 3), (3, 1)


def shift(value, da=0, db=0, dx=(0, 0), dc=0):
    pairs = []
    for z in range(NZ):
        for x in range(NX):
            for c in range(NC):
                source = (z * NX + x) * NC + c
                to_z = (z + 2 * da) % NZ ^ db
                pairs.append((source, (to_z * NX + (x ^ dx[c])) * NC + (c ^ dc)))
    return lax.ppermute(value, "dp", pairs)


def along_z(value):
    rest = NX * NC
    groups = [[z * rest + i for z in range(NZ)] for i in range(rest)]
    return lax.all_to_all(
        value, "dp", split_axis=0, concat_axis=0, tiled=True, axis_index_groups=groups
    )


def sum_over(value, axis):
    copies = jnp.broadcast_to(value, (lax.axis_size(axis), 8, 128))
    parts = lax.all_to_all(copies, axis, split_axis=0, concat_axis=0, tiled=True)
    return jnp.sum(parts[:, 0, 0])


def iota(shape, axis):
    return lax.broadcasted_iota(jnp.int32, shape, axis).astype(F32)


def route_kernel(rows_ref, master_ref, first_ref, second_ref, out_ref):
    count = rows_ref.shape[1]
    rows_dev = float(count)
    along = rows_ref[...].astype(F32)
    line, column = iota((count, count), 0), iota((count, count), 1)
    down = jnp.sum(jnp.where(line == column, along, 0.0), axis=1, keepdims=True)
    owner_down = jnp.sum(
        jnp.where(down >= rows_dev * (iota((count, 128), 1) + 1.0), 1.0, 0.0), axis=1, keepdims=True
    )
    owner_along = jnp.sum(
        jnp.where(along >= rows_dev * (iota((DP, count), 0) + 1.0), 1.0, 0.0), axis=0, keepdims=True
    )
    before = jnp.where((owner_down == owner_along) & (line < column), 1.0, 0.0)
    within = jnp.sum(before, axis=0, keepdims=True)
    code = owner_along * CAP + within
    pick = jnp.where(code == iota((DP * CAP, count), 0), 1.0, 0.0).astype(BF16)
    label = jnp.broadcast_to(down - rows_dev * owner_down + 1.0, (count, 128))
    data = jnp.concatenate(
        [master_ref[...], first_ref[...], second_ref[...], label], axis=1
    ).astype(BF16)
    sent = jnp.dot(pick, data, preferred_element_type=F32)
    parts = [sent[:, 128 * k : 128 * k + 128].reshape(DP, CAP, 128) for k in range(4)]
    out_ref[...] = jnp.concatenate(parts, axis=1).astype(BF16)


def route(rows, master, first, second):
    return pl.pallas_call(
        route_kernel,
        out_shape=jax.ShapeDtypeStruct((DP, 4 * CAP, 128), BF16),
        name="route",
    )(rows.reshape(1, -1), master, first, second)


def place_kernel(box_ref, weight_ref, first_ref, second_ref):
    box = box_ref[...].astype(F32)
    parts = [box[:, CAP * k : CAP * k + CAP, :].reshape(DP * CAP, 128) for k in range(4)]
    label = parts[3]
    lane = iota((DP * CAP, 128), 1)
    pick = jnp.concatenate(
        [jnp.where(label == lane + 1.0, 1.0, 0.0), jnp.where(label == lane + 129.0, 1.0, 0.0)],
        axis=1,
    ).astype(BF16)
    data = jnp.concatenate(parts[:3], axis=1).astype(BF16)
    placed = lax.dot_general(
        pick, data, (((0,), (0,)), ((), ())), preferred_element_type=F32
    )
    weight_ref[...] = placed[:PAD, :128].astype(BF16)
    first_ref[...] = placed[:PAD, 128:256]
    second_ref[...] = placed[:PAD, 256:384]


def place(box):
    return pl.pallas_call(
        place_kernel,
        out_shape=(
            jax.ShapeDtypeStruct((PAD, 128), BF16),
            jax.ShapeDtypeStruct((PAD, 128), F32),
            jax.ShapeDtypeStruct((PAD, 128), F32),
        ),
        name="place",
    )(box)


def pick_of(key, values):
    chosen = jnp.int32(values[-1])
    for index, value in enumerate(values[:-1]):
        chosen = jnp.where(key == index, jnp.int32(value), chosen)
    return chosen


def fetch(tokens_hbm, tokens_ref, sems):
    width = tokens_ref.shape[1] // BLOCKS
    copies = [
        pltpu.make_async_copy(
            tokens_hbm.at[:, pl.ds(i * width, width)],
            tokens_ref.at[:, pl.ds(i * width, width)],
            sems.at[i],
        )
        for i in range(BLOCKS)
    ]
    for copy in copies:
        copy.start()
    return copies


def grad_kernel(
    rows_dev, me_ref, cot_ref, tokens_hbm, send_ref, keep_ref, tokens_ref, whole_ref, sems
):
    features = tokens_ref.shape[1]
    width = features // BLOCKS
    copies = fetch(tokens_hbm, tokens_ref, sems)
    my_x, even = lax.rem(lax.div(me_ref[0], NC), NX), lax.rem(me_ref[0], NC) == 0
    whole_ref[features:, :] = jnp.zeros((whole_ref.shape[0] - features, 128), F32)
    turned = cot_ref[...].T
    chip = 0
    for i in range(BLOCKS):
        copies[i].wait()
        across = jnp.dot(
            turned, tokens_ref[:, i * width : i * width + width], preferred_element_type=F32
        )
        whole_ref[i * width : i * width + width, :] = across.T
        ready = (i + 1) * width if i < BLOCKS - 1 else whole_ref.shape[0]
        while chip < DP // NC and (2 * chip + 1) * rows_dev + PAD <= ready:
            z, x = chip // NX, chip % NX
            apart = jnp.bitwise_xor(my_x, x)
            zero, one = pick_of(apart, (18, 6, 0, 12)), pick_of(apart, (18, 12, 0, 6))
            kept = z + jnp.where(even, zero, one)
            sent = z + jnp.where(even, one, zero)
            first = whole_ref[2 * chip * rows_dev : 2 * chip * rows_dev + PAD, :]
            second = whole_ref[(2 * chip + 1) * rows_dev : (2 * chip + 1) * rows_dev + PAD, :]
            keep_ref[kept] = jnp.where(even, first, second)
            send_ref[sent] = jnp.where(even, second, first).astype(BF16)
            chip += 1


def grad(me, cotangent, tokens, rows_dev):
    _, features = tokens.shape
    return pl.pallas_call(
        functools.partial(grad_kernel, rows_dev),
        out_shape=(
            jax.ShapeDtypeStruct((24, PAD, 128), BF16),
            jax.ShapeDtypeStruct((24, PAD, 128), F32),
        ),
        in_specs=[
            pl.BlockSpec(memory_space=pltpu.SMEM),
            pl.BlockSpec(memory_space=pltpu.VMEM),
            pl.BlockSpec(memory_space=pltpu.HBM),
        ],
        out_specs=[pl.BlockSpec(memory_space=pltpu.VMEM)] * 2,
        scratch_shapes=[
            pltpu.VMEM(tokens.shape, BF16),
            pltpu.VMEM((features + 32, 128), F32),
            pltpu.SemaphoreType.DMA((BLOCKS,)),
        ],
        compiler_params=pltpu.CompilerParams(vmem_limit_bytes=60_000_000),
        name="grad",
    )(me.reshape(1), cotangent, tokens)


def apply_kernel(
    rows_dev, me_ref, mine_ref, other_ref, tokens_hbm, out_ref, tokens_ref, rows_ref, sems
):
    features = tokens_ref.shape[1]
    width = features // BLOCKS
    copies = fetch(tokens_hbm, tokens_ref, sems)
    my_z = lax.div(me_ref[0], NX * NC)
    my_x, even = lax.rem(lax.div(me_ref[0], NC), NX), lax.rem(me_ref[0], NC) == 0
    total = jnp.zeros(out_ref.shape, F32)
    chip = 0
    for i in range(BLOCKS):
        while chip < DP // NC and 2 * chip * rows_dev < (i + 1) * width:
            z, x = chip // NX, chip % NX
            back = lax.rem(lax.div(my_z, 2) + 3 - z // 2, 3)
            back += jnp.where(lax.rem(my_z, 2) == z % 2, 0, 3)
            apart = jnp.bitwise_xor(my_x, x)
            zero, one = pick_of(apart, (0, 6, 18, 12)), pick_of(apart, (0, 12, 18, 6))
            mine = mine_ref[back + jnp.where(even, zero, one)].astype(F32)
            other = other_ref[back + jnp.where(even, one, zero)].astype(F32)
            start = 2 * chip * rows_dev
            rows_ref[start : start + PAD, :] = jnp.where(even, mine, other)
            start += rows_dev
            rows_ref[start : start + PAD, :] = jnp.where(even, other, mine)
            chip += 1
        block = slice(i * width, i * width + width)
        copies[i].wait()
        total += jnp.dot(
            tokens_ref[:, block], rows_ref[block, :].astype(BF16), preferred_element_type=F32
        )
    out_ref[...] = total.astype(BF16)


def apply(me, mine, other, tokens, rows_dev):
    tall, features = tokens.shape
    return pl.pallas_call(
        functools.partial(apply_kernel, rows_dev),
        out_shape=jax.ShapeDtypeStruct((tall, 128), BF16),
        in_specs=[pl.BlockSpec(memory_space=pltpu.SMEM)]
        + [pl.BlockSpec(memory_space=pltpu.VMEM)] * 2
        + [pl.BlockSpec(memory_space=pltpu.HBM)],
        scratch_shapes=[
            pltpu.VMEM(tokens.shape, BF16),
            pltpu.VMEM((features + 32, 128), F32),
            pltpu.SemaphoreType.DMA((BLOCKS,)),
        ],
        compiler_params=pltpu.CompilerParams(vmem_limit_bytes=60_000_000),
        name="apply",
    )(me.reshape(1), mine, other, tokens)


def per_device(tokens, cotangent, master, first_moment, second_moment, old_rows):
    rows_dev = master.shape[0]
    me = lax.axis_index("dp")

    box = route(old_rows, master, first_moment, second_moment)
    arrived = lax.all_to_all(box, "dp", split_axis=0, concat_axis=0, tiled=True)
    weight_own, first, second = place(arrived)

    send, keep = grad(me, cotangent, tokens, rows_dev)
    got = shift(send, dc=1)
    next_x = (keep[:12] + got[:12].astype(F32)).astype(BF16)
    got_x = shift(next_x, dx=FIRST)
    next_x = keep[12:18] + got[12:18].astype(F32) + got_x[:6].astype(F32)
    next_x = next_x.astype(BF16)
    next_x, got_x = lax.optimization_barrier((next_x, got_x))
    last_x = shift(next_x, dx=SECOND)
    sums = keep[18:] + got[18:].astype(F32) + got_x[6:].astype(F32) + last_x.astype(F32)
    sums = sums.astype(BF16)
    got_z = along_z(sums)
    gradient = jnp.sum(got_z.astype(F32), axis=0)[:rows_dev]

    one = shift(weight_own, da=1)
    two = shift(weight_own, da=2)
    run = jnp.stack([weight_own, one, two])
    beside = shift(run, db=1)
    run = jnp.concatenate([run, beside], axis=0)
    west = shift(run, dx=FIRST)
    pair = jnp.concatenate([run, west], axis=0)
    rest = shift(pair, dx=SECOND)
    mine = jnp.concatenate([pair, rest], axis=0)
    other = shift(mine, dc=1)

    squares = jnp.sum(gradient * gradient)
    squares = sum_over(squares, "tensor")
    squares = sum_over(squares, "dp")
    keys_values = apply(me, mine, other, tokens, rows_dev)

    factor = clip_norm / (jnp.sqrt(squares) + 1e-06)
    clipped = gradient * factor
    moment_one = beta_one * first[:rows_dev] + (1.0 - beta_one) * clipped
    moment_two = beta_two * second[:rows_dev] + (1.0 - beta_two) * clipped * clipped
    update = moment_one / (jnp.sqrt(moment_two) + adam_eps)
    return (keys_values, update)


def solution(mesh):
    in_specs = (
        P("dp", None),
        P("dp", "tensor"),
        P("dp", "tensor"),
        P("dp", "tensor"),
        P("dp", "tensor"),
        P("dp"),
    )
    out_specs = (P("dp", "tensor"), P("dp", "tensor"))
    return jax.shard_map(
        per_device, mesh=mesh, in_specs=in_specs, out_specs=out_specs, check_vma=False
    )
```

```python
import functools

import jax
import jax.numpy as jnp
from jax import lax
from jax.experimental import pallas as pl
from jax.experimental.pallas import tpu as pltpu
from jax.sharding import Mesh
from jax.sharding import PartitionSpec as P

beta_one = 0.9
beta_two = 0.95
adam_eps = 1e-08
clip_norm = 1.0

F32, BF16 = jnp.float32, jnp.bfloat16
NZ, NX, NC = 6, 4, 2
DP = NZ * NX * NC
CAP = 8
ROWS = ("z", "x", "core")
PAD = 176
BLOCKS = 8


FIRST, SECOND = (1, 3), (3, 1)


def shift(value, dx=(0, 0), dc=0):
    pairs = []
    for z in range(NZ):
        for x in range(NX):
            for c in range(NC):
                source = (z * NX + x) * NC + c
                pairs.append((source, (z * NX + (x ^ dx[c])) * NC + (c ^ dc)))
    return lax.ppermute(value, ROWS, pairs)


def along_z(value):
    return lax.all_to_all(value, "z", split_axis=0, concat_axis=0, tiled=True)


def sum_over(value, axes):
    copies = jnp.broadcast_to(value, (lax.axis_size(axes), 8, 128))
    parts = lax.all_to_all(copies, axes, split_axis=0, concat_axis=0, tiled=True)
    return jnp.sum(parts[:, 0, 0])


def iota(shape, axis):
    return lax.broadcasted_iota(jnp.int32, shape, axis).astype(F32)


def route_kernel(rows_ref, master_ref, first_ref, second_ref, out_ref):
    count = rows_ref.shape[1]
    rows_dev = float(count)
    along = rows_ref[...].astype(F32)
    line, column = iota((count, count), 0), iota((count, count), 1)
    down = jnp.sum(jnp.where(line == column, along, 0.0), axis=1, keepdims=True)
    owner_down = jnp.sum(
        jnp.where(down >= rows_dev * (iota((count, 128), 1) + 1.0), 1.0, 0.0), axis=1, keepdims=True
    )
    owner_along = jnp.sum(
        jnp.where(along >= rows_dev * (iota((DP, count), 0) + 1.0), 1.0, 0.0), axis=0, keepdims=True
    )
    before = jnp.where((owner_down == owner_along) & (line < column), 1.0, 0.0)
    within = jnp.sum(before, axis=0, keepdims=True)
    code = owner_along * CAP + within
    pick = jnp.where(code == iota((DP * CAP, count), 0), 1.0, 0.0).astype(BF16)
    label = jnp.broadcast_to(down - rows_dev * owner_down + 1.0, (count, 128))
    data = jnp.concatenate(
        [master_ref[...], first_ref[...], second_ref[...], label], axis=1
    ).astype(BF16)
    sent = jnp.dot(pick, data, preferred_element_type=F32)
    parts = [sent[:, 128 * k : 128 * k + 128].reshape(DP, CAP, 128) for k in range(4)]
    out_ref[...] = jnp.concatenate(parts, axis=1).astype(BF16)


def route(rows, master, first, second):
    return pl.pallas_call(
        route_kernel,
        out_shape=jax.ShapeDtypeStruct((DP, 4 * CAP, 128), BF16),
        name="route",
    )(rows.reshape(1, -1), master, first, second)


def place_kernel(box_ref, weight_ref, first_ref, second_ref):
    box = box_ref[...].astype(F32)
    parts = [box[:, CAP * k : CAP * k + CAP, :].reshape(DP * CAP, 128) for k in range(4)]
    label = parts[3]
    lane = iota((DP * CAP, 128), 1)
    pick = jnp.concatenate(
        [jnp.where(label == lane + 1.0, 1.0, 0.0), jnp.where(label == lane + 129.0, 1.0, 0.0)],
        axis=1,
    ).astype(BF16)
    data = jnp.concatenate(parts[:3], axis=1).astype(BF16)
    placed = lax.dot_general(
        pick, data, (((0,), (0,)), ((), ())), preferred_element_type=F32
    )
    weight = placed[:PAD, :128].astype(BF16)
    for z in range(NZ):
        weight_ref[z] = weight
    first_ref[...] = placed[:PAD, 128:256]
    second_ref[...] = placed[:PAD, 256:384]


def place(box):
    return pl.pallas_call(
        place_kernel,
        out_shape=(
            jax.ShapeDtypeStruct((NZ, PAD, 128), BF16),
            jax.ShapeDtypeStruct((PAD, 128), F32),
            jax.ShapeDtypeStruct((PAD, 128), F32),
        ),
        name="place",
    )(box)


def pick_of(key, values):
    chosen = jnp.int32(values[-1])
    for index, value in enumerate(values[:-1]):
        chosen = jnp.where(key == index, jnp.int32(value), chosen)
    return chosen


def fetch(tokens_hbm, tokens_ref, sems):
    width = tokens_ref.shape[1] // BLOCKS
    copies = [
        pltpu.make_async_copy(
            tokens_hbm.at[:, pl.ds(i * width, width)],
            tokens_ref.at[:, pl.ds(i * width, width)],
            sems.at[i],
        )
        for i in range(BLOCKS)
    ]
    for copy in copies:
        copy.start()
    return copies


def grad_kernel(
    rows_dev, me_ref, cot_ref, tokens_hbm, send_ref, keep_ref, tokens_ref, whole_ref, sems
):
    features = tokens_ref.shape[1]
    width = features // BLOCKS
    copies = fetch(tokens_hbm, tokens_ref, sems)
    my_x, even = lax.rem(lax.div(me_ref[0], NC), NX), lax.rem(me_ref[0], NC) == 0
    whole_ref[features:, :] = jnp.zeros((whole_ref.shape[0] - features, 128), F32)
    turned = cot_ref[...].T
    chip = 0
    for i in range(BLOCKS):
        copies[i].wait()
        across = jnp.dot(
            turned, tokens_ref[:, i * width : i * width + width], preferred_element_type=F32
        )
        whole_ref[i * width : i * width + width, :] = across.T
        ready = (i + 1) * width if i < BLOCKS - 1 else whole_ref.shape[0]
        while chip < DP // NC and (2 * chip + 1) * rows_dev + PAD <= ready:
            z, x = chip // NX, chip % NX
            apart = jnp.bitwise_xor(my_x, x)
            zero, one = pick_of(apart, (18, 6, 0, 12)), pick_of(apart, (18, 12, 0, 6))
            kept = z + jnp.where(even, zero, one)
            sent = z + jnp.where(even, one, zero)
            first = whole_ref[2 * chip * rows_dev : 2 * chip * rows_dev + PAD, :]
            second = whole_ref[(2 * chip + 1) * rows_dev : (2 * chip + 1) * rows_dev + PAD, :]
            keep_ref[kept] = jnp.where(even, first, second).astype(BF16)
            send_ref[sent] = jnp.where(even, second, first).astype(BF16)
            chip += 1


def grad(me, cotangent, tokens, rows_dev):
    _, features = tokens.shape
    return pl.pallas_call(
        functools.partial(grad_kernel, rows_dev),
        out_shape=(
            jax.ShapeDtypeStruct((24, PAD, 128), BF16),
            jax.ShapeDtypeStruct((24, PAD, 128), BF16),
        ),
        in_specs=[
            pl.BlockSpec(memory_space=pltpu.SMEM),
            pl.BlockSpec(memory_space=pltpu.VMEM),
            pl.BlockSpec(memory_space=pltpu.HBM),
        ],
        out_specs=[pl.BlockSpec(memory_space=pltpu.VMEM)] * 2,
        scratch_shapes=[
            pltpu.VMEM(tokens.shape, BF16),
            pltpu.VMEM((features + 32, 128), F32),
            pltpu.SemaphoreType.DMA((BLOCKS,)),
        ],
        compiler_params=pltpu.CompilerParams(vmem_limit_bytes=60_000_000),
        name="grad",
    )(me.reshape(1), cotangent, tokens)


def apply_kernel(
    rows_dev,
    me_ref,
    mine_ref,
    other_hbm,
    tokens_hbm,
    out_ref,
    other_ref,
    tokens_ref,
    rows_ref,
    sems,
    row_sem,
):
    features = tokens_ref.shape[1]
    width = features // BLOCKS
    gathered = pltpu.make_async_copy(other_hbm, other_ref, row_sem)
    gathered.start()
    copies = fetch(tokens_hbm, tokens_ref, sems)
    gathered.wait()
    my_x, even = lax.rem(lax.div(me_ref[0], NC), NX), lax.rem(me_ref[0], NC) == 0
    total = jnp.zeros(out_ref.shape, F32)
    chip = 0
    for i in range(BLOCKS):
        while chip < DP // NC and 2 * chip * rows_dev < (i + 1) * width:
            z, x = chip // NX, chip % NX
            apart = jnp.bitwise_xor(my_x, x)
            zero, one = pick_of(apart, (0, 6, 18, 12)), pick_of(apart, (0, 12, 18, 6))
            mine = mine_ref[z + jnp.where(even, zero, one)].astype(F32)
            other = other_ref[z + jnp.where(even, one, zero)].astype(F32)
            start = 2 * chip * rows_dev
            rows_ref[start : start + PAD, :] = jnp.where(even, mine, other)
            start += rows_dev
            rows_ref[start : start + PAD, :] = jnp.where(even, other, mine)
            chip += 1
        block = slice(i * width, i * width + width)
        copies[i].wait()
        total += jnp.dot(
            tokens_ref[:, block], rows_ref[block, :].astype(BF16), preferred_element_type=F32
        )
    out_ref[...] = total.astype(BF16)


def apply(me, mine, other, tokens, rows_dev):
    tall, features = tokens.shape
    return pl.pallas_call(
        functools.partial(apply_kernel, rows_dev),
        out_shape=jax.ShapeDtypeStruct((tall, 128), BF16),
        in_specs=[pl.BlockSpec(memory_space=pltpu.SMEM)]
        + [pl.BlockSpec(memory_space=pltpu.VMEM)]
        + [pl.BlockSpec(memory_space=pltpu.HBM)] * 2,
        scratch_shapes=[
            pltpu.VMEM(other.shape, BF16),
            pltpu.VMEM(tokens.shape, BF16),
            pltpu.VMEM((features + 32, 128), F32),
            pltpu.SemaphoreType.DMA((BLOCKS,)),
            pltpu.SemaphoreType.DMA,
        ],
        compiler_params=pltpu.CompilerParams(vmem_limit_bytes=65_200_000),
        name="apply",
    )(me.reshape(1), mine, other, tokens)


def per_device(tokens, cotangent, master, first_moment, second_moment, old_rows):
    rows_dev = master.shape[0]
    me = lax.axis_index(ROWS)

    box = route(old_rows, master, first_moment, second_moment)
    arrived = lax.all_to_all(box, ROWS, split_axis=0, concat_axis=0, tiled=True)
    weight_own, first, second = place(arrived)

    send, keep = grad(me, cotangent, tokens, rows_dev)
    got = shift(send, dc=1)
    next_x = (keep[:12].astype(F32) + got[:12].astype(F32)).astype(BF16)
    got_x = shift(next_x, dx=FIRST)
    next_x = keep[12:18].astype(F32) + got[12:18].astype(F32) + got_x[:6].astype(F32)
    next_x = next_x.astype(BF16)
    next_x, got_x = lax.optimization_barrier((next_x, got_x))
    last_x = shift(next_x, dx=SECOND)
    sums = keep[18:].astype(F32) + got[18:].astype(F32) + got_x[6:].astype(F32) + last_x.astype(F32)
    got_z = along_z(sums.astype(BF16))
    gradient = jnp.sum(got_z.astype(F32), axis=0)[:rows_dev]

    run = along_z(weight_own)
    west = shift(run, dx=FIRST)
    pair = jnp.concatenate([run, west], axis=0)
    rest = shift(pair, dx=SECOND)
    mine = jnp.concatenate([pair, rest], axis=0)
    other = shift(mine, dc=1)

    squares = jnp.sum(gradient * gradient)
    squares = sum_over(squares, ("z", "far"))
    squares = sum_over(squares, ("x", "core", "y"))
    keys_values = apply(me, mine, other, tokens, rows_dev)

    factor = clip_norm / (jnp.sqrt(squares) + 1e-06)
    clipped = gradient * factor
    moment_one = beta_one * first[:rows_dev] + (1.0 - beta_one) * clipped
    moment_two = beta_two * second[:rows_dev] + (1.0 - beta_two) * clipped * clipped
    update = moment_one / (jnp.sqrt(moment_two) + adam_eps)
    return (keys_values, update)


def solution(mesh):
    rows, columns = ROWS, ("far", "y")
    fine = Mesh(mesh.devices.reshape(NZ, NX, NC, 2, -1), rows + columns)
    in_specs = (
        P(rows, None),
        P(rows, columns),
        P(rows, columns),
        P(rows, columns),
        P(rows, columns),
        P(rows),
    )
    out_specs = (P(rows, columns), P(rows, columns))
    return jax.shard_map(
        per_device, mesh=fine, in_specs=in_specs, out_specs=out_specs, check_vma=False
    )
```

```python
import functools

import jax
import jax.numpy as jnp
from jax import lax
from jax.experimental import pallas as pl
from jax.experimental.pallas import tpu as pltpu
from jax.sharding import Mesh
from jax.sharding import PartitionSpec as P

beta_one = 0.9
beta_two = 0.95
adam_eps = 1e-08
clip_norm = 1.0

F32, BF16 = jnp.float32, jnp.bfloat16
NZ, NX, NC = 6, 4, 2
DP = NZ * NX * NC
CAP = 8
ROWS = ("z", "x", "core")
PAD = 176
BLOCKS = 8
AHEAD = 3


FIRST, SECOND = (1, 3), (3, 1)


def shift(value, dx=(0, 0), dc=0):
    pairs = []
    for z in range(NZ):
        for x in range(NX):
            for c in range(NC):
                source = (z * NX + x) * NC + c
                pairs.append((source, (z * NX + (x ^ dx[c])) * NC + (c ^ dc)))
    return lax.ppermute(value, ROWS, pairs)


def along_z(value):
    return lax.all_to_all(value, "z", split_axis=0, concat_axis=0, tiled=True)


def sum_over(value, axes):
    copies = jnp.broadcast_to(value, (lax.axis_size(axes), 8, 128))
    parts = lax.all_to_all(copies, axes, split_axis=0, concat_axis=0, tiled=True)
    return jnp.sum(parts[:, 0, 0])


def iota(shape, axis):
    return lax.broadcasted_iota(jnp.int32, shape, axis).astype(F32)


def route_kernel(rows_ref, master_ref, first_ref, second_ref, out_ref):
    count = rows_ref.shape[1]
    rows_dev = float(count)
    along = rows_ref[...].astype(F32)
    line, column = iota((count, count), 0), iota((count, count), 1)
    down = jnp.sum(jnp.where(line == column, along, 0.0), axis=1, keepdims=True)
    owner_down = jnp.sum(
        jnp.where(down >= rows_dev * (iota((count, 128), 1) + 1.0), 1.0, 0.0), axis=1, keepdims=True
    )
    owner_along = jnp.sum(
        jnp.where(along >= rows_dev * (iota((DP, count), 0) + 1.0), 1.0, 0.0), axis=0, keepdims=True
    )
    before = jnp.where((owner_down == owner_along) & (line < column), 1.0, 0.0)
    within = jnp.sum(before, axis=0, keepdims=True)
    code = owner_along * CAP + within
    pick = jnp.where(code == iota((DP * CAP, count), 0), 1.0, 0.0).astype(BF16)
    label = jnp.broadcast_to(down - rows_dev * owner_down + 1.0, (count, 128))
    data = jnp.concatenate(
        [master_ref[...], first_ref[...], second_ref[...], label], axis=1
    ).astype(BF16)
    sent = jnp.dot(pick, data, preferred_element_type=F32)
    parts = [sent[:, 128 * k : 128 * k + 128].reshape(DP, CAP, 128) for k in range(4)]
    out_ref[...] = jnp.concatenate(parts, axis=1).astype(BF16)


def route(rows, master, first, second):
    return pl.pallas_call(
        route_kernel,
        out_shape=jax.ShapeDtypeStruct((DP, 4 * CAP, 128), BF16),
        name="route",
    )(rows.reshape(1, -1), master, first, second)


def place_kernel(box_ref, weight_ref, first_ref, second_ref):
    box = box_ref[...].astype(F32)
    parts = [box[:, CAP * k : CAP * k + CAP, :].reshape(DP * CAP, 128) for k in range(4)]
    label = parts[3]
    lane = iota((DP * CAP, 128), 1)
    pick = jnp.concatenate(
        [jnp.where(label == lane + 1.0, 1.0, 0.0), jnp.where(label == lane + 129.0, 1.0, 0.0)],
        axis=1,
    ).astype(BF16)
    data = jnp.concatenate(parts[:3], axis=1).astype(BF16)
    placed = lax.dot_general(
        pick, data, (((0,), (0,)), ((), ())), preferred_element_type=F32
    )
    weight = placed[:PAD, :128].astype(BF16)
    for z in range(NZ):
        weight_ref[z] = weight
    first_ref[...] = placed[:PAD, 128:256]
    second_ref[...] = placed[:PAD, 256:384]


def place(box):
    return pl.pallas_call(
        place_kernel,
        out_shape=(
            jax.ShapeDtypeStruct((NZ, PAD, 128), BF16),
            jax.ShapeDtypeStruct((PAD, 128), F32),
            jax.ShapeDtypeStruct((PAD, 128), F32),
        ),
        name="place",
    )(box)


def pick_of(key, values):
    chosen = jnp.int32(values[-1])
    for index, value in enumerate(values[:-1]):
        chosen = jnp.where(key == index, jnp.int32(value), chosen)
    return chosen


def fetch(tokens_hbm, tokens_ref, sems):
    width = tokens_ref.shape[1] // BLOCKS
    copies = [
        pltpu.make_async_copy(
            tokens_hbm.at[:, pl.ds(i * width, width)],
            tokens_ref.at[:, pl.ds(i * width, width)],
            sems.at[i],
        )
        for i in range(BLOCKS)
    ]
    for copy in copies[:AHEAD]:
        copy.start()
    return copies


def take(copies, index):
    copies[index].wait()
    if index + AHEAD < len(copies):
        copies[index + AHEAD].start()


def grad_kernel(
    rows_dev, me_ref, cot_ref, tokens_hbm, send_ref, keep_ref, tokens_ref, whole_ref, sems
):
    features = tokens_ref.shape[1]
    width = features // BLOCKS
    copies = fetch(tokens_hbm, tokens_ref, sems)
    my_x, even = lax.rem(lax.div(me_ref[0], NC), NX), lax.rem(me_ref[0], NC) == 0
    whole_ref[features:, :] = jnp.zeros((whole_ref.shape[0] - features, 128), F32)
    turned = cot_ref[...].T
    chip = 0
    for i in range(BLOCKS):
        take(copies, i)
        across = jnp.dot(
            turned, tokens_ref[:, i * width : i * width + width], preferred_element_type=F32
        )
        whole_ref[i * width : i * width + width, :] = across.T
        ready = (i + 1) * width if i < BLOCKS - 1 else whole_ref.shape[0]
        while chip < DP // NC and (2 * chip + 1) * rows_dev + PAD <= ready:
            z, x = chip // NX, chip % NX
            apart = jnp.bitwise_xor(my_x, x)
            zero, one = pick_of(apart, (18, 6, 0, 12)), pick_of(apart, (18, 12, 0, 6))
            kept = z + jnp.where(even, zero, one)
            sent = z + jnp.where(even, one, zero)
            first = whole_ref[2 * chip * rows_dev : 2 * chip * rows_dev + PAD, :]
            second = whole_ref[(2 * chip + 1) * rows_dev : (2 * chip + 1) * rows_dev + PAD, :]
            keep_ref[kept] = jnp.where(even, first, second).astype(BF16)
            send_ref[sent] = jnp.where(even, second, first).astype(BF16)
            chip += 1


def grad(me, cotangent, tokens, rows_dev):
    _, features = tokens.shape
    return pl.pallas_call(
        functools.partial(grad_kernel, rows_dev),
        out_shape=(
            jax.ShapeDtypeStruct((24, PAD, 128), BF16),
            jax.ShapeDtypeStruct((24, PAD, 128), BF16),
        ),
        in_specs=[
            pl.BlockSpec(memory_space=pltpu.SMEM),
            pl.BlockSpec(memory_space=pltpu.VMEM),
            pl.BlockSpec(memory_space=pltpu.HBM),
        ],
        out_specs=[pl.BlockSpec(memory_space=pltpu.VMEM)] * 2,
        scratch_shapes=[
            pltpu.VMEM(tokens.shape, BF16),
            pltpu.VMEM((features + 32, 128), F32),
            pltpu.SemaphoreType.DMA((BLOCKS,)),
        ],
        compiler_params=pltpu.CompilerParams(vmem_limit_bytes=60_000_000),
        name="grad",
    )(me.reshape(1), cotangent, tokens)


def apply_kernel(
    rows_dev,
    me_ref,
    mine_ref,
    other_hbm,
    tokens_hbm,
    out_ref,
    other_ref,
    tokens_ref,
    rows_ref,
    sems,
    row_sems,
):
    features = tokens_ref.shape[1]
    width = features // BLOCKS
    my_x, even = lax.rem(lax.div(me_ref[0], NC), NX), lax.rem(me_ref[0], NC) == 0
    places, gathered = [], []
    for chip in range(DP // NC):
        z, x = chip // NX, chip % NX
        apart = jnp.bitwise_xor(my_x, x)
        zero, one = pick_of(apart, (0, 6, 18, 12)), pick_of(apart, (0, 12, 18, 6))
        places.append(z + jnp.where(even, zero, one))
        gathered.append(
            pltpu.make_async_copy(
                other_hbm.at[z + jnp.where(even, one, zero)],
                other_ref.at[chip],
                row_sems.at[chip],
            )
        )
        gathered[chip].start()
    copies = fetch(tokens_hbm, tokens_ref, sems)
    total = jnp.zeros(out_ref.shape, F32)
    chip = 0
    for i in range(BLOCKS):
        while chip < DP // NC and 2 * chip * rows_dev < (i + 1) * width:
            gathered[chip].wait()
            mine, other = mine_ref[places[chip]].astype(F32), other_ref[chip].astype(F32)
            start = 2 * chip * rows_dev
            rows_ref[start : start + PAD, :] = jnp.where(even, mine, other)
            start += rows_dev
            rows_ref[start : start + PAD, :] = jnp.where(even, other, mine)
            chip += 1
        block = slice(i * width, i * width + width)
        take(copies, i)
        total += jnp.dot(
            tokens_ref[:, block], rows_ref[block, :].astype(BF16), preferred_element_type=F32
        )
    out_ref[...] = total.astype(BF16)


def apply(me, mine, other, tokens, rows_dev):
    tall, features = tokens.shape
    return pl.pallas_call(
        functools.partial(apply_kernel, rows_dev),
        out_shape=jax.ShapeDtypeStruct((tall, 128), BF16),
        in_specs=[pl.BlockSpec(memory_space=pltpu.SMEM)]
        + [pl.BlockSpec(memory_space=pltpu.VMEM)]
        + [pl.BlockSpec(memory_space=pltpu.HBM)] * 2,
        scratch_shapes=[
            pltpu.VMEM(other.shape, BF16),
            pltpu.VMEM(tokens.shape, BF16),
            pltpu.VMEM((features + 32, 128), F32),
            pltpu.SemaphoreType.DMA((BLOCKS,)),
            pltpu.SemaphoreType.DMA((DP // NC,)),
        ],
        compiler_params=pltpu.CompilerParams(vmem_limit_bytes=65_200_000),
        name="apply",
    )(me.reshape(1), mine, other, tokens)


def per_device(tokens, cotangent, master, first_moment, second_moment, old_rows):
    rows_dev = master.shape[0]
    me = lax.axis_index(ROWS)

    box = route(old_rows, master, first_moment, second_moment)
    arrived = lax.all_to_all(box, ROWS, split_axis=0, concat_axis=0, tiled=True)
    weight_own, first, second = place(arrived)

    send, keep = grad(me, cotangent, tokens, rows_dev)
    got = shift(send, dc=1)
    next_x = (keep[:12].astype(F32) + got[:12].astype(F32)).astype(BF16)
    got_x = shift(next_x, dx=FIRST)
    next_x = keep[12:18].astype(F32) + got[12:18].astype(F32) + got_x[:6].astype(F32)
    next_x = next_x.astype(BF16)
    next_x, got_x = lax.optimization_barrier((next_x, got_x))
    last_x = shift(next_x, dx=SECOND)
    sums = keep[18:].astype(F32) + got[18:].astype(F32) + got_x[6:].astype(F32) + last_x.astype(F32)
    got_z = along_z(sums.astype(BF16))
    gradient = jnp.sum(got_z.astype(F32), axis=0)[:rows_dev]

    run = along_z(weight_own)
    west = shift(run, dx=FIRST)
    pair = jnp.concatenate([run, west], axis=0)
    rest = shift(pair, dx=SECOND)
    mine = jnp.concatenate([pair, rest], axis=0)
    other = shift(mine, dc=1)

    squares = jnp.sum(gradient * gradient)
    squares = sum_over(squares, ("z", "far"))
    squares = sum_over(squares, ("x", "core", "y"))
    keys_values = apply(me, mine, other, tokens, rows_dev)

    factor = clip_norm / (jnp.sqrt(squares) + 1e-06)
    clipped = gradient * factor
    moment_one = beta_one * first[:rows_dev] + (1.0 - beta_one) * clipped
    moment_two = beta_two * second[:rows_dev] + (1.0 - beta_two) * clipped * clipped
    update = moment_one / (jnp.sqrt(moment_two) + adam_eps)
    return (keys_values, update)


def solution(mesh):
    rows, columns = ROWS, ("far", "y")
    fine = Mesh(mesh.devices.reshape(NZ, NX, NC, 2, -1), rows + columns)
    in_specs = (
        P(rows, None),
        P(rows, columns),
        P(rows, columns),
        P(rows, columns),
        P(rows, columns),
        P(rows),
    )
    out_specs = (P(rows, columns), P(rows, columns))
    return jax.shard_map(
        per_device, mesh=fine, in_specs=in_specs, out_specs=out_specs, check_vma=False
    )
```

```python
import functools

import jax
import jax.numpy as jnp
from jax import lax
from jax.experimental import pallas as pl
from jax.experimental.pallas import tpu as pltpu
from jax.sharding import Mesh
from jax.sharding import PartitionSpec as P

beta_one = 0.9
beta_two = 0.95
adam_eps = 1e-08
clip_norm = 1.0

F32, BF16 = jnp.float32, jnp.bfloat16
NZ, NX, NC = 6, 4, 2
DP = NZ * NX * NC
CAP = 8
ROWS = ("z", "x", "core")
PAD = 176
BLOCKS = 8
AHEAD = 3


FIRST, SECOND = (1, 3), (3, 1)


def shift(value, dx=(0, 0), dc=0):
    pairs = []
    for z in range(NZ):
        for x in range(NX):
            for c in range(NC):
                source = (z * NX + x) * NC + c
                pairs.append((source, (z * NX + (x ^ dx[c])) * NC + (c ^ dc)))
    return lax.ppermute(value, ROWS, pairs)


def along_z(value):
    return lax.all_to_all(value, "z", split_axis=0, concat_axis=0, tiled=True)


def sum_over(lanes, axes):
    copies = jnp.broadcast_to(lanes, (lax.axis_size(axes), 8, 128))
    parts = lax.all_to_all(copies, axes, split_axis=0, concat_axis=0, tiled=True)
    return jnp.sum(parts, axis=0)


def iota(shape, axis):
    return lax.broadcasted_iota(jnp.int32, shape, axis).astype(F32)


def route_kernel(rows_ref, master_ref, first_ref, second_ref, out_ref):
    count = rows_ref.shape[1]
    rows_dev = float(count)
    along = rows_ref[...].astype(F32)
    line, column = iota((count, count), 0), iota((count, count), 1)
    down = jnp.sum(jnp.where(line == column, along, 0.0), axis=1, keepdims=True)
    owner_down = jnp.sum(
        jnp.where(down >= rows_dev * (iota((count, 128), 1) + 1.0), 1.0, 0.0), axis=1, keepdims=True
    )
    owner_along = jnp.sum(
        jnp.where(along >= rows_dev * (iota((DP, count), 0) + 1.0), 1.0, 0.0), axis=0, keepdims=True
    )
    before = jnp.where((owner_down == owner_along) & (line < column), 1.0, 0.0)
    within = jnp.sum(before, axis=0, keepdims=True)
    code = owner_along * CAP + within
    pick = jnp.where(code == iota((DP * CAP, count), 0), 1.0, 0.0).astype(BF16)
    label = jnp.broadcast_to(down - rows_dev * owner_down + 1.0, (count, 128))
    data = jnp.concatenate(
        [master_ref[...], first_ref[...], second_ref[...], label], axis=1
    ).astype(BF16)
    sent = jnp.dot(pick, data, preferred_element_type=F32)
    parts = [sent[:, 128 * k : 128 * k + 128].reshape(DP, CAP, 128) for k in range(4)]
    out_ref[...] = jnp.concatenate(parts, axis=1).astype(BF16)


def route(rows, master, first, second):
    return pl.pallas_call(
        route_kernel,
        out_shape=jax.ShapeDtypeStruct((DP, 4 * CAP, 128), BF16),
        name="route",
    )(rows.reshape(1, -1), master, first, second)


def place_kernel(box_ref, weight_ref, first_ref, second_ref):
    box = box_ref[...].astype(F32)
    parts = [box[:, CAP * k : CAP * k + CAP, :].reshape(DP * CAP, 128) for k in range(4)]
    label = parts[3]
    lane = iota((DP * CAP, 128), 1)
    pick = jnp.concatenate(
        [jnp.where(label == lane + 1.0, 1.0, 0.0), jnp.where(label == lane + 129.0, 1.0, 0.0)],
        axis=1,
    ).astype(BF16)
    data = jnp.concatenate(parts[:3], axis=1).astype(BF16)
    placed = lax.dot_general(
        pick, data, (((0,), (0,)), ((), ())), preferred_element_type=F32
    )
    weight = placed[:PAD, :128].astype(BF16)
    for z in range(NZ):
        weight_ref[z] = weight
    first_ref[...] = placed[:PAD, 128:256]
    second_ref[...] = placed[:PAD, 256:384]


def place(box):
    return pl.pallas_call(
        place_kernel,
        out_shape=(
            jax.ShapeDtypeStruct((NZ, PAD, 128), BF16),
            jax.ShapeDtypeStruct((PAD, 128), F32),
            jax.ShapeDtypeStruct((PAD, 128), F32),
        ),
        name="place",
    )(box)


def pick_of(key, values):
    chosen = jnp.int32(values[-1])
    for index, value in enumerate(values[:-1]):
        chosen = jnp.where(key == index, jnp.int32(value), chosen)
    return chosen


def fetch(tokens_hbm, tokens_ref, sems):
    width = tokens_ref.shape[1] // BLOCKS
    copies = [
        pltpu.make_async_copy(
            tokens_hbm.at[:, pl.ds(i * width, width)],
            tokens_ref.at[:, pl.ds(i * width, width)],
            sems.at[i],
        )
        for i in range(BLOCKS)
    ]
    for copy in copies[:AHEAD]:
        copy.start()
    return copies


def take(copies, index):
    copies[index].wait()
    if index + AHEAD < len(copies):
        copies[index + AHEAD].start()


def grad_kernel(
    rows_dev, me_ref, cot_ref, tokens_hbm, send_ref, keep_ref, tokens_ref, whole_ref, sems
):
    features = tokens_ref.shape[1]
    width = features // BLOCKS
    copies = fetch(tokens_hbm, tokens_ref, sems)
    my_x, even = lax.rem(lax.div(me_ref[0], NC), NX), lax.rem(me_ref[0], NC) == 0
    whole_ref[features:, :] = jnp.zeros((whole_ref.shape[0] - features, 128), F32)
    turned = cot_ref[...].T
    chip = 0
    for i in range(BLOCKS):
        take(copies, i)
        across = jnp.dot(
            turned, tokens_ref[:, i * width : i * width + width], preferred_element_type=F32
        )
        whole_ref[i * width : i * width + width, :] = across.T
        ready = (i + 1) * width if i < BLOCKS - 1 else whole_ref.shape[0]
        while chip < DP // NC and (2 * chip + 1) * rows_dev + PAD <= ready:
            z, x = chip // NX, chip % NX
            apart = jnp.bitwise_xor(my_x, x)
            zero, one = pick_of(apart, (18, 6, 0, 12)), pick_of(apart, (18, 12, 0, 6))
            kept = z + jnp.where(even, zero, one)
            sent = z + jnp.where(even, one, zero)
            first = whole_ref[2 * chip * rows_dev : 2 * chip * rows_dev + PAD, :]
            second = whole_ref[(2 * chip + 1) * rows_dev : (2 * chip + 1) * rows_dev + PAD, :]
            keep_ref[kept] = jnp.where(even, first, second).astype(BF16)
            send_ref[sent] = jnp.where(even, second, first).astype(BF16)
            chip += 1


def grad(me, cotangent, tokens, rows_dev):
    _, features = tokens.shape
    return pl.pallas_call(
        functools.partial(grad_kernel, rows_dev),
        out_shape=(
            jax.ShapeDtypeStruct((24, PAD, 128), BF16),
            jax.ShapeDtypeStruct((24, PAD, 128), BF16),
        ),
        in_specs=[
            pl.BlockSpec(memory_space=pltpu.SMEM),
            pl.BlockSpec(memory_space=pltpu.VMEM),
            pl.BlockSpec(memory_space=pltpu.HBM),
        ],
        out_specs=[pl.BlockSpec(memory_space=pltpu.VMEM)] * 2,
        scratch_shapes=[
            pltpu.VMEM(tokens.shape, BF16),
            pltpu.VMEM((features + 32, 128), F32),
            pltpu.SemaphoreType.DMA((BLOCKS,)),
        ],
        compiler_params=pltpu.CompilerParams(vmem_limit_bytes=60_000_000),
        name="grad",
    )(me.reshape(1), cotangent, tokens)


def apply_kernel(
    rows_dev,
    me_ref,
    mine_ref,
    other_hbm,
    tokens_hbm,
    out_ref,
    other_ref,
    tokens_ref,
    rows_ref,
    sems,
    row_sems,
):
    features = tokens_ref.shape[1]
    width = features // BLOCKS
    my_x, even = lax.rem(lax.div(me_ref[0], NC), NX), lax.rem(me_ref[0], NC) == 0
    places, gathered = [], []
    for chip in range(DP // NC):
        z, x = chip // NX, chip % NX
        apart = jnp.bitwise_xor(my_x, x)
        zero, one = pick_of(apart, (0, 6, 18, 12)), pick_of(apart, (0, 12, 18, 6))
        places.append(z + jnp.where(even, zero, one))
        gathered.append(
            pltpu.make_async_copy(
                other_hbm.at[z + jnp.where(even, one, zero)],
                other_ref.at[chip],
                row_sems.at[chip],
            )
        )
        gathered[chip].start()
    copies = fetch(tokens_hbm, tokens_ref, sems)
    total = jnp.zeros(out_ref.shape, F32)
    chip = 0
    for i in range(BLOCKS):
        while chip < DP // NC and 2 * chip * rows_dev < (i + 1) * width:
            gathered[chip].wait()
            mine, other = mine_ref[places[chip]].astype(F32), other_ref[chip].astype(F32)
            start = 2 * chip * rows_dev
            rows_ref[start : start + PAD, :] = jnp.where(even, mine, other)
            start += rows_dev
            rows_ref[start : start + PAD, :] = jnp.where(even, other, mine)
            chip += 1
        block = slice(i * width, i * width + width)
        take(copies, i)
        total += jnp.dot(
            tokens_ref[:, block], rows_ref[block, :].astype(BF16), preferred_element_type=F32
        )
    out_ref[...] = total.astype(BF16)


def apply(me, mine, other, tokens, rows_dev):
    tall, features = tokens.shape
    return pl.pallas_call(
        functools.partial(apply_kernel, rows_dev),
        out_shape=jax.ShapeDtypeStruct((tall, 128), BF16),
        in_specs=[pl.BlockSpec(memory_space=pltpu.SMEM)]
        + [pl.BlockSpec(memory_space=pltpu.VMEM)]
        + [pl.BlockSpec(memory_space=pltpu.HBM)] * 2,
        scratch_shapes=[
            pltpu.VMEM(other.shape, BF16),
            pltpu.VMEM(tokens.shape, BF16),
            pltpu.VMEM((features + 32, 128), F32),
            pltpu.SemaphoreType.DMA((BLOCKS,)),
            pltpu.SemaphoreType.DMA((DP // NC,)),
        ],
        compiler_params=pltpu.CompilerParams(vmem_limit_bytes=65_200_000),
        name="apply",
    )(me.reshape(1), mine, other, tokens)


def per_device(tokens, cotangent, master, first_moment, second_moment, old_rows):
    rows_dev = master.shape[0]
    me = lax.axis_index(ROWS)

    box = route(old_rows, master, first_moment, second_moment)
    arrived = lax.all_to_all(box, ROWS, split_axis=0, concat_axis=0, tiled=True)
    weight_own, first, second = place(arrived)

    send, keep = grad(me, cotangent, tokens, rows_dev)
    got = shift(send, dc=1)
    next_x = (keep[:12].astype(F32) + got[:12].astype(F32)).astype(BF16)
    got_x = shift(next_x, dx=FIRST)
    next_x = keep[12:18].astype(F32) + got[12:18].astype(F32) + got_x[:6].astype(F32)
    next_x = next_x.astype(BF16)
    next_x, got_x = lax.optimization_barrier((next_x, got_x))
    last_x = shift(next_x, dx=SECOND)
    sums = keep[18:].astype(F32) + got[18:].astype(F32) + got_x[6:].astype(F32) + last_x.astype(F32)
    got_z = along_z(sums.astype(BF16))
    gradient = jnp.sum(got_z.astype(F32), axis=0)[:rows_dev]

    run = along_z(weight_own)
    west = shift(run, dx=FIRST)
    pair = jnp.concatenate([run, west], axis=0)
    rest = shift(pair, dx=SECOND)
    mine = jnp.concatenate([pair, rest], axis=0)
    other = shift(mine, dc=1)

    squares = jnp.sum(gradient * gradient, axis=0)
    squares = sum_over(squares, ("z", "core", "far"))
    squares = sum_over(squares, ("x", "y"))
    keys_values = apply(me, mine, other, tokens, rows_dev)

    factor = clip_norm / (jnp.sqrt(jnp.sum(squares) / 8.0) + 1e-06)
    clipped = gradient * factor
    moment_one = beta_one * first[:rows_dev] + (1.0 - beta_one) * clipped
    moment_two = beta_two * second[:rows_dev] + (1.0 - beta_two) * clipped * clipped
    update = moment_one / (jnp.sqrt(moment_two) + adam_eps)
    return (keys_values, update)


def solution(mesh):
    rows, columns = ROWS, ("far", "y")
    fine = Mesh(mesh.devices.reshape(NZ, NX, NC, 2, -1), rows + columns)
    in_specs = (
        P(rows, None),
        P(rows, columns),
        P(rows, columns),
        P(rows, columns),
        P(rows, columns),
        P(rows),
    )
    out_specs = (P(rows, columns), P(rows, columns))
    return jax.shard_map(
        per_device, mesh=fine, in_specs=in_specs, out_specs=out_specs, check_vma=False
    )
```
